32 devices in a mesh: ctx: 4 (over x, core), fsdp: 8 (over z, y).
Axes of the slice: x: 2, y: 2, z: 4, core: 2. Of those that a mesh axis runs over, the one named last changes fastest.
Arguments:
- hidden: bfloat16 [16, 1024, 3, 1024], P('fsdp', 'ctx'), may hold values from -6 to 6
- encoded: bfloat16 [16, 512, 1024], P('fsdp', 'ctx'), may hold values from -6 to 6
- assign: int32 [32], replicated, may hold values from 0 to 31, as said below
- bucket_table: int32 [1055], replicated, may hold values from 0 to 31
- w_query: bfloat16 [1024, 1024], P('fsdp'), may hold values from -0.1875 to 0.1875
- w_key: bfloat16 [1024, 1024], P('fsdp'), may hold values from -0.1875 to 0.1875
- w_value: bfloat16 [1024, 1024], P('fsdp'), may hold values from -0.1875 to 0.1875
- w_rel: bfloat16 [1024, 512], P('fsdp'), may hold values from -0.1875 to 0.1875
- w_out: bfloat16 [1024, 1024], P('fsdp'), may hold values from -0.75 to 0.75
- gain_one: bfloat16 [1024], P('fsdp'), may hold values from 0.25 to 1.75
- shift_one: bfloat16 [1024], P('fsdp'), may hold values from -3 to 3
- c_query: bfloat16 [1024, 1024], P('fsdp'), may hold values from -0.1875 to 0.1875
- c_key: bfloat16 [1024, 1024], P('fsdp'), may hold values from -0.1875 to 0.1875
- c_value: bfloat16 [1024, 1024], P('fsdp'), may hold values from -0.1875 to 0.1875
- c_out: bfloat16 [1024, 1024], P('fsdp'), may hold values from -3 to 3
- gain_two: bfloat16 [1024], P('fsdp'), may hold values from 0.25 to 1.75
- shift_two: bfloat16 [1024], P('fsdp'), may hold values from -3 to 3
- w_inner: bfloat16 [1024, 4096], P('fsdp'), may hold values from -0.1875 to 0.1875
- w_outer: bfloat16 [4096, 1024], P('fsdp'), may hold values from -0.09375 to 0.09375
- gain_three: bfloat16 [1024], P('fsdp'), may hold values from 0.25 to 1.75
- shift_three: bfloat16 [1024], P('fsdp'), may hold values from -3 to 3
- cotangent: bfloat16 [16, 1024, 3, 1024], P('fsdp', 'ctx'), may hold values from -6 to 6
Outputs:
- output: bfloat16 [16, 1024, 3, 1024], P('fsdp', 'ctx')
- grad_hidden: float32 [16, 1024, 3, 1024], P('fsdp', 'ctx')
- grad_encoded: float32 [16, 512, 1024], P('fsdp', 'ctx')
- grad_w_query: float32 [1024, 1024], P('fsdp')
- grad_w_key: float32 [1024, 1024], P('fsdp')
- grad_w_value: float32 [1024, 1024], P('fsdp')
- grad_w_rel: float32 [1024, 512], P('fsdp')
- grad_w_out: float32 [1024, 1024], P('fsdp')
- grad_gain_one: float32 [1024], P('fsdp')
- grad_shift_one: float32 [1024], P('fsdp')
- grad_c_query: float32 [1024, 1024], P('fsdp')
- grad_c_key: float32 [1024, 1024], P('fsdp')
- grad_c_value: float32 [1024, 1024], P('fsdp')
- grad_c_out: float32 [1024, 1024], P('fsdp')
- grad_gain_two: float32 [1024], P('fsdp')
- grad_shift_two: float32 [1024], P('fsdp')
- grad_w_inner: float32 [1024, 4096], P('fsdp')
- grad_w_outer: float32 [4096, 1024], P('fsdp')
- grad_gain_three: float32 [1024], P('fsdp')
- grad_shift_three: float32 [1024], P('fsdp')
The draws below stay inside these ranges and needn't reach their ends.
Inputs may be any that keep to these rules, and one draw needn't show every extreme that they name: assign holds each of the 32 block numbers once; slots 2 i and 2 i + 1 hold blocks b and 31 - b, in either order.
All inputs are finite; a program needn't handle non-finite values.
Results may differ from the reference program's by a relative error of at most 0.03.
Values may be sent and summed in bfloat16 or wider, within the bound.
No kernel may reach another device: no remote copies, remote signals or barrier semaphores. Data moves between devices by JAX's collectives and lax.ppermute only.
A program may use at most 640 MiB of HBM per device.

```python
import math
import jax
import jax.numpy as jnp
from jax import lax

D = 1024
HEADS = 16
HEAD_DIM = 64
FF = 4096
BUCKETS = 32
BLK = 32
SEQ = 1024
ENC = 512
STREAMS = 3
SEQS = 16
NB = 32
SPAN = 1055


def draw_assign(key, part):
    order = jax.random.permutation(jax.random.fold_in(key, 11), NB // 2)
    flips = jax.random.randint(jax.random.fold_in(key, 12), (NB // 2,), 0, 2)
    first = jnp.where(flips == 1, NB - 1 - order, order)
    return jnp.stack([first, NB - 1 - first], axis=1).reshape(NB).astype(jnp.int32)


def plant(drawn, rng, smallest, high):
    longest = drawn.shape.index(max(drawn.shape))
    spots = []
    for shift in (0, 1):
        where = [jax.random.randint(jax.random.fold_in(rng, axis), (), 0, length) for axis, length in enumerate(drawn.shape)]
        where[longest] = (where[longest] + shift) % drawn.shape[longest]
        spots.append(tuple(where))
    return drawn.at[spots[0]].set(smallest).at[spots[1]].set(high)


def block_scale(stream_key, dims, cuts, low, top_value):
    loudness, own = 1.0, jax.random.fold_in(stream_key, 6)
    for dim, blocks in cuts:
        steps = jnp.exp(jax.random.uniform(jax.random.fold_in(own, dim), (blocks,), jnp.float32, low / len(cuts), top_value / len(cuts)))
        loudness = loudness * jnp.repeat(steps, dims[dim] // blocks).reshape([-1 if axis == dim else 1 for axis in range(len(dims))])
    return loudness


def noise(own_key, shape, scale, bound, cuts=(), kind=jnp.bfloat16):
    loudness = block_scale(own_key, shape, cuts, -0.22, 0.18) if cuts else 1.0
    entries = jax.random.normal(own_key, shape, jnp.float32) * scale * loudness
    return jnp.minimum(jnp.maximum(entries, -bound), bound).astype(kind)


def setup_inputs(seed: int = 0) -> dict:
    key_of = jax.random.split(jax.random.key(seed), 23)
    return {
        "hidden": noise(key_of[0], (SEQS, SEQ, STREAMS, D), 1.0, 6.0, ((0, 8), (1, 4))),
        "encoded": noise(key_of[1], (SEQS, ENC, D), 1.0, 6.0, ((0, 8), (1, 4))),
        "assign": draw_assign(jax.random.fold_in(key_of[22], 71), 0),
        "bucket_table": plant(jax.random.randint(key_of[3], (SPAN,), 0, BUCKETS), jax.random.fold_in(key_of[3], 1), 0, BUCKETS - 1).astype(jnp.int32),
        "w_query": noise(key_of[4], (D, D), D ** -0.5, 0.1875, ((0, 8),)),
        "w_key": noise(key_of[5], (D, D), D ** -0.5, 0.1875, ((0, 8),)),
        "w_value": noise(key_of[6], (D, D), D ** -0.5, 0.1875, ((0, 8),)),
        "w_rel": noise(key_of[7], (D, BUCKETS * HEADS), D ** -0.5, 0.1875, ((0, 8),)),
        "w_out": noise(key_of[8], (D, D), (D // 16) ** -0.5, 0.75, ((0, 8),)),
        "gain_one": jnp.clip(1.0 + 0.15 * jax.random.normal(key_of[9], (D,), jnp.float32), 0.25, 1.75).astype(jnp.bfloat16),
        "shift_one": noise(key_of[10], (D,), 0.5, 3.0, ((0, 8),)),
        "c_query": noise(key_of[11], (D, D), D ** -0.5, 0.1875, ((0, 8),)),
        "c_key": noise(key_of[12], (D, D), D ** -0.5, 0.1875, ((0, 8),)),
        "c_value": noise(key_of[13], (D, D), D ** -0.5, 0.1875, ((0, 8),)),
        "c_out": noise(key_of[14], (D, D), (max(D // 256, 1)) ** -0.5, 3.0, ((0, 8),)),
        "gain_two": jnp.clip(1.0 + 0.15 * jax.random.normal(key_of[15], (D,), jnp.float32), 0.25, 1.75).astype(jnp.bfloat16),
        "shift_two": noise(key_of[16], (D,), 0.5, 3.0, ((0, 8),)),
        "w_inner": noise(key_of[17], (D, FF), D ** -0.5, 0.1875, ((0, 8),)),
        "w_outer": noise(key_of[18], (FF, D), FF ** -0.5, 0.09375, ((0, 8),)),
        "gain_three": jnp.clip(1.0 + 0.15 * jax.random.normal(key_of[19], (D,), jnp.float32), 0.25, 1.75).astype(jnp.bfloat16),
        "shift_three": noise(key_of[20], (D,), 0.5, 3.0, ((0, 8),)),
        "cotangent": noise(key_of[21], (SEQS, SEQ, STREAMS, D), 1.0, 6.0, ((0, 8), (1, 4))),
    }


HIGHEST_PRECISION = lax.Precision.HIGHEST
EPSILON = 1e-05
FILLER = -1e+30

@jax.custom_vjp
def low(v):
    return lax.optimization_barrier(v.astype(jnp.bfloat16)).astype(jnp.float32)

@jax.custom_vjp
def low_back(v):
    return v

def low_keep(v):
    return (low(v), None)

def low_pass(kept, grad):
    return (grad,)

def back_keep(v):
    return (v, None)

def back_low(kept, grad):
    return (low(grad),)
low.defvjp(low_keep, low_pass)
low_back.defvjp(back_keep, back_low)

def project(left, right):
    return jnp.dot(left, right, precision=HIGHEST_PRECISION, preferred_element_type=jnp.float32)

def layer_norm(values, gain, shift):
    average = lax.optimization_barrier(jnp.mean(values, axis=-1, keepdims=True))
    centred = values - average
    variance = lax.optimization_barrier(jnp.mean(centred * centred, axis=-1, keepdims=True))
    return centred * lax.rsqrt(variance + EPSILON) * gain + shift

def forward(params, rows, encoded_rows, blocks, places, bucket_table):
    w_query, w_key, w_value, w_rel, w_out, gain_one, shift_one, c_query, c_key, c_value, c_out, gain_two, shift_two, w_inner, w_outer, gain_three, shift_three = params
    scale = HEAD_DIM ** (-0.5)
    length = rows.shape[0]
    streams = rows.shape[1]
    flat = rows.reshape(length * streams, D)
    query = low(low_back(project(flat, w_query))).reshape(length, streams, HEADS, HEAD_DIM)
    keys = low(low_back(project(flat, w_key))).reshape(length, streams, HEADS, HEAD_DIM)
    values = low(low_back(project(flat, w_value))).reshape(length, streams, HEADS, HEAD_DIM)
    rel = low(low_back(project(flat, w_rel))).reshape(length, streams, BUCKETS, HEADS)
    keys_main = keys[:, 0]
    values_main = values[:, 0]
    own_bucket = bucket_table[BLK - 1]
    span = bucket_table.shape[0]
    block_rows = math.gcd(length, 256)
    block_count = length // block_rows
    has_own = (jnp.arange(streams) > 0)[:, None, None]

    def self_block(pieces):
        query_b, rel_b, keys_b, values_b, blocks_b, places_b = pieces
        raw = jnp.einsum('rshd,khd->shrk', query_b, keys_main, precision=HIGHEST_PRECISION) * scale
        distance = jnp.clip(places_b[:, None] - places[None, :] + BLK - 1, 0, span - 1)
        buckets = bucket_table[distance]
        picked = rel_b[jnp.arange(block_rows)[:, None], :, buckets, :]
        scores = low_back(raw + jnp.transpose(picked, (2, 3, 0, 1)))
        allowed = blocks_b[:, None] >= blocks[None, :]
        masked = jnp.where(allowed, scores, FILLER)
        own_raw = jnp.einsum('rshd,rshd->shr', query_b, keys_b, precision=HIGHEST_PRECISION) * scale
        own_scores = low_back(own_raw + jnp.transpose(rel_b[:, :, own_bucket, :], (1, 2, 0)))
        own_masked = jnp.where(has_own, own_scores, FILLER)
        top = jnp.maximum(lax.optimization_barrier(jnp.max(masked, axis=-1)), own_masked)
        weights_k = jnp.exp(masked - top[..., None])
        own_weight = jnp.exp(own_masked - top)
        total = lax.optimization_barrier(jnp.sum(weights_k, axis=-1)) + own_weight
        probs = low(weights_k / total[..., None])
        own_prob = low(own_weight / total)
        mixed = jnp.einsum('shrk,khd->rshd', probs, values_main, precision=HIGHEST_PRECISION)
        mixed = mixed + jnp.transpose(own_prob, (2, 0, 1))[..., None] * values_b
        return low(low_back(mixed))
    pieces = (query.reshape(block_count, block_rows, streams, HEADS, HEAD_DIM), rel.reshape(block_count, block_rows, streams, BUCKETS, HEADS), keys.reshape(block_count, block_rows, streams, HEADS, HEAD_DIM), values.reshape(block_count, block_rows, streams, HEADS, HEAD_DIM), blocks.reshape(block_count, block_rows), places.reshape(block_count, block_rows))
    mixed = lax.map(jax.checkpoint(self_block), pieces).reshape(length * streams, D)
    attn_out = low_back(project(mixed, w_out))
    h_one = layer_norm(flat + attn_out, gain_one, shift_one)
    cross_query = low(low_back(project(low(h_one), c_query)))
    enc_keys = low(low_back(project(encoded_rows, c_key))).reshape(-1, HEADS, HEAD_DIM)
    enc_values = low(low_back(project(encoded_rows, c_value))).reshape(-1, HEADS, HEAD_DIM)
    total_rows = length * streams
    cross_rows = math.gcd(total_rows, 512)
    cross_count = total_rows // cross_rows

    def cross_block(query_b):
        scores = low_back(jnp.einsum('nhd,khd->hnk', query_b, enc_keys, precision=HIGHEST_PRECISION) * scale)
        top = lax.optimization_barrier(jnp.max(scores, axis=-1))
        weights_k = jnp.exp(scores - top[..., None])
        total = lax.optimization_barrier(jnp.sum(weights_k, axis=-1))
        probs = low(weights_k / total[..., None])
        mixed_b = jnp.einsum('hnk,khd->nhd', probs, enc_values, precision=HIGHEST_PRECISION)
        return low(low_back(mixed_b))
    cross_mixed = lax.map(jax.checkpoint(cross_block), cross_query.reshape(cross_count, cross_rows, HEADS, HEAD_DIM)).reshape(total_rows, D)
    cross_out = low_back(project(cross_mixed, c_out))
    h_two = layer_norm(h_one + cross_out, gain_two, shift_two)
    inner = low_back(project(low(h_two), w_inner))
    active = low(jax.nn.gelu(inner, approximate=False))
    ffn_out = low_back(project(active, w_outer))
    result = layer_norm(h_two + ffn_out, gain_three, shift_three)
    return result.reshape(length, streams, D)

def reference(hidden, encoded, assign, bucket_table, w_query, w_key, w_value, w_rel, w_out, gain_one, shift_one, c_query, c_key, c_value, c_out, gain_two, shift_two, w_inner, w_outer, gain_three, shift_three, cotangent):
    weights = tuple((item.astype(jnp.float32) for item in (w_query, w_key, w_value, w_rel, w_out, gain_one, shift_one, c_query, c_key, c_value, c_out, gain_two, shift_two, w_inner, w_outer, gain_three, shift_three)))
    blocks = jnp.broadcast_to(assign[:, None], (assign.shape[0], BLK)).reshape(-1).astype(jnp.int32)
    places = (blocks * BLK + jnp.arange(blocks.shape[0], dtype=jnp.int32) % BLK).astype(jnp.int32)

    def one_sequence(carry, pieces):
        rows, encoded_rows, cotangent_rows = pieces

        def apply(params, values, encoder_values):
            return forward(params, values, encoder_values, blocks, places, bucket_table)
        result, pullback = jax.vjp(apply, weights, rows.astype(jnp.float32), encoded_rows.astype(jnp.float32))
        grad_params, grad_rows, grad_enc = pullback(cotangent_rows.astype(jnp.float32))
        carry = jax.tree.map(jnp.add, carry, grad_params)
        return (carry, (result.astype(jnp.bfloat16), grad_rows, grad_enc))
    start = tuple((jnp.zeros(item.shape, jnp.float32) for item in weights))
    totals, outputs = lax.scan(one_sequence, start, (hidden, encoded, cotangent))
    return (outputs[0], outputs[1], outputs[2], totals[0], totals[1], totals[2], totals[3], totals[4], totals[5], totals[6], totals[7], totals[8], totals[9], totals[10], totals[11], totals[12], totals[13], totals[14], totals[15], totals[16])
```

```python
import functools
import jax
import jax.numpy as jnp
from jax import lax
from jax.sharding import PartitionSpec as P
from jax.experimental import pallas as pl
from jax.experimental.pallas import tpu as pltpu

HEAD_DIM = 64
BUCKETS = 32
BLK = 32
CHUNK = 256
FILLER = -1e30
SCALE = HEAD_DIM ** (-0.5)
LIMIT = 60 * 1024 * 1024
F32 = jnp.float32
BF16 = jnp.bfloat16


def dot_nt(left, right):
    return lax.dot_general(left, right, (((1,), (1,)), ((), ())), preferred_element_type=F32)


def dot_tn(left, right):
    return lax.dot_general(left, right, (((0,), (0,)), ((), ())), preferred_element_type=F32)


def dot_nn(left, right):
    return jnp.dot(left, right, preferred_element_type=F32)


def low_lanes(rows):
    return lax.broadcasted_iota(jnp.int32, (rows, 128), 1) < HEAD_DIM


def pair_rows(value, low):
    zero = jnp.zeros_like(value)
    return jnp.concatenate([jnp.where(low, value, zero), jnp.where(low, zero, value)], axis=0)


def self_parts(place, query_ref, own_key_ref, own_value_ref):
    slot, pair = place // 2, place % 2
    rows = pl.ds(pl.multiple_of(slot * BLK, BLK), BLK)
    lanes = pl.ds(pl.multiple_of(pair * 128, 128), 128)
    total = query_ref.shape[0] * BLK
    low = low_lanes(total)
    query = query_ref[:, 0, rows, lanes].reshape(total, 128)
    pairs = pair_rows(query, low) * jnp.asarray(SCALE, BF16)
    zero = jnp.zeros((BLK, 128), F32)
    own_key = own_key_ref[:, 0, rows, lanes].reshape(total - BLK, 128).astype(F32)
    own_key = jnp.concatenate([zero, own_key], axis=0)
    own_value = own_value_ref[:, 0, rows, lanes].reshape(total - BLK, 128).astype(F32)
    own_value = jnp.concatenate([zero, own_value], axis=0)
    return slot, pair, rows, lanes, low, pairs, own_key, own_value


def self_forward_kernel(
    blocks,
    own_ref,
    query_ref,
    rel_ref,
    own_key_ref,
    own_value_ref,
    key_ref,
    value_ref,
    index_ref,
    out_ref,
    prob_ref,
    own_prob_ref,
):
    seq = key_ref.shape[1]
    streams = query_ref.shape[0]
    total = streams * BLK

    def step(place, carry):
        slot, pair, rows, lanes, low, pairs, own_key, own_value = self_parts(
            place, query_ref, own_key_ref, own_value_ref
        )
        block = blocks[slot]
        rel = rel_ref[:, 0, rows, :].reshape(total, 128).astype(F32)
        table = jnp.concatenate(
            [pltpu.roll(rel, pair * 64, 1), pltpu.roll(rel, pair * 64 + 96, 1)], axis=0
        )
        lane = lax.broadcasted_iota(jnp.int32, (2 * total, 128), 1)
        own = jnp.where(lane == own_ref[0], table, 0.0)
        own = own + pairs.astype(F32) * jnp.concatenate([own_key, own_key], axis=0)
        own = jnp.sum(own, axis=1, keepdims=True)
        row = lax.broadcasted_iota(jnp.int32, (2 * total, 1), 0)
        main = jnp.logical_or(row < BLK, jnp.logical_and(row >= total, row < total + BLK))
        own = jnp.where(main, FILLER, own)
        count = (block * BLK) // CHUNK + 1
        for parts in range(1, seq // CHUNK + 1):
            width = parts * CHUNK

            @pl.when(count == parts)
            def _():
                span = slice(seq - width, seq)
                index = index_ref[rows, span]
                bias = [
                    jnp.take_along_axis(
                        table,
                        jnp.concatenate([index[:, start : start + 128]] * (2 * streams), axis=0),
                        axis=1,
                    )
                    for start in range(0, width, 128)
                ]
                scores = dot_nt(pairs, key_ref[0, span, lanes]) + jnp.concatenate(bias, axis=1)
                column = lax.broadcasted_iota(jnp.int32, (2 * total, CHUNK), 1)
                seen = column >= width - BLK * (block + 1)
                first = jnp.where(seen, scores[:, :CHUNK], FILLER)
                scores = (
                    jnp.concatenate([first, scores[:, CHUNK:]], axis=1) if parts > 1 else first
                )
                top = jnp.maximum(jnp.max(scores, axis=1, keepdims=True), own)
                weights = jnp.exp(scores - top)
                own_weight = jnp.exp(own - top)
                inverse = 1.0 / (jnp.sum(weights, axis=1, keepdims=True) + own_weight)
                probs = (weights * inverse).astype(BF16)
                prob_ref[0, pair, slot, :, span] = probs
                own_prob = own_weight * inverse
                own_prob_ref[0, pair, slot] = jnp.broadcast_to(own_prob, (2 * total, 128)).astype(
                    BF16
                )
                mixed = dot_nn(probs, value_ref[0, span, lanes])
                result = jnp.where(
                    low,
                    mixed[:total] + own_prob[:total] * own_value,
                    mixed[total:] + own_prob[total:] * own_value,
                )
                out_ref[:, 0, rows, lanes] = result.astype(BF16).reshape(streams, BLK, 128)

        return carry

    lax.fori_loop(0, 2 * blocks.shape[0], step, 0)


def self_backward_kernel(
    blocks,
    own_ref,
    query_ref,
    own_key_ref,
    own_value_ref,
    key_ref,
    value_ref,
    hot_ref,
    out_ref,
    grad_ref,
    prob_ref,
    own_prob_ref,
    grad_query_ref,
    grad_rel_ref,
    grad_own_key_ref,
    grad_own_value_ref,
    grad_key_ref,
    grad_value_ref,
    key_total,
    value_total,
):
    seq = key_ref.shape[1]
    streams = query_ref.shape[0]
    total = streams * BLK
    key_total[...] = jnp.zeros_like(key_total)
    value_total[...] = jnp.zeros_like(value_total)

    def step(place, carry):
        slot, pair, rows, lanes, low, pairs, own_key, own_value = self_parts(
            place, query_ref, own_key_ref, own_value_ref
        )
        block = blocks[slot]
        grads = pair_rows(grad_ref[:, 0, rows, lanes].reshape(total, 128), low)
        wide = grads.astype(F32)
        mixed = out_ref[:, 0, rows, lanes].reshape(total, 128).astype(F32)
        delta = jnp.sum(wide * jnp.concatenate([mixed, mixed], axis=0), axis=1, keepdims=True)
        grad_own = jnp.sum(
            wide * jnp.concatenate([own_value, own_value], axis=0), axis=1, keepdims=True
        )
        own_prob = own_prob_ref[0, pair, slot].astype(F32)
        grad_own = own_prob * (grad_own - delta)
        part = grad_own * pairs.astype(F32)
        part = (part[:total] + part[total:])[BLK:]
        grad_own_key_ref[:, 0, rows, lanes] = part.astype(BF16).reshape(streams - 1, BLK, 128)
        part = own_prob * wide
        part = (part[:total] + part[total:])[BLK:]
        grad_own_value_ref[:, 0, rows, lanes] = part.astype(BF16).reshape(streams - 1, BLK, 128)
        count = (block * BLK) // CHUNK + 1
        for parts in range(1, seq // CHUNK + 1):
            width = parts * CHUNK

            @pl.when(count == parts)
            def _():
                span = slice(seq - width, seq)
                probs = prob_ref[0, pair, slot, :, span]
                grad_probs = dot_nt(grads, value_ref[0, span, lanes])
                grad_scores = probs.astype(F32) * (grad_probs - delta)
                low_scores = grad_scores.astype(BF16)
                value_total[span, lanes] += dot_tn(probs, grads)
                key_total[span, lanes] += dot_tn(low_scores, pairs)
                moved = dot_nn(low_scores, key_ref[0, span, lanes])
                moved = jnp.where(
                    low,
                    moved[:total] + grad_own[:total] * own_key,
                    moved[total:] + grad_own[total:] * own_key,
                )
                grad_query_ref[:, 0, rows, lanes] = (
                    (moved * SCALE).astype(BF16).reshape(streams, BLK, 128)
                )
                pad = jnp.zeros((BLK, 128), F32)
                skewed = []
                for start in range(0, 2 * total, BLK):
                    piece = jnp.concatenate([grad_scores[start : start + BLK], pad], axis=1)
                    skewed.append(pltpu.roll(piece, 0, 1, stride=1, stride_axis=0).astype(BF16))
                begin = pl.multiple_of(BLK * (block + 1) - width + CHUNK, BLK)
                hots = hot_ref[pl.ds(begin, width + 128), :]
                sums = dot_nn(jnp.concatenate(skewed, axis=0), hots)
                lane = lax.broadcasted_iota(jnp.int32, (2 * total, 128), 1)
                sums = sums + jnp.where(lane == own_ref[0], grad_own, 0.0)
                sums = pltpu.roll(sums[:total], pair * 64, 1) + pltpu.roll(
                    sums[total:], pair * 64 + BUCKETS, 1
                )
                lane = lax.broadcasted_iota(jnp.int32, (total, 128), 1)
                mine = jnp.logical_and(lane >= 64 * pair, lane < 64 * pair + 64)
                before = grad_rel_ref[:, 0, rows, :].reshape(total, 128)
                sums = jnp.where(mine, sums.astype(BF16), before)
                grad_rel_ref[:, 0, rows, :] = sums.reshape(streams, BLK, 128)

        return carry

    lax.fori_loop(0, 2 * blocks.shape[0], step, 0)
    grad_key_ref[0] = key_total[...].astype(BF16)
    grad_value_ref[0] = value_total[...].astype(BF16)


def group_spec(streams, rows, lanes):
    return pl.BlockSpec((streams, 1, rows, lanes), lambda n, g: (0, n, 0, g))


def full_spec(rows, lanes):
    return pl.BlockSpec((1, rows, lanes), lambda n, g: (n, 0, g))


def smem_spec():
    return pl.BlockSpec(memory_space=pltpu.SMEM)


def estimate(flops, moved):
    return pl.CostEstimate(flops=int(flops), bytes_accessed=int(moved), transcendentals=0)


def prob_spec(slots, total, width):
    return pl.BlockSpec((1, 2, slots, total, width), lambda n, g: (n, g, 0, 0, 0))


def whole_spec(value):
    return pl.BlockSpec(value.shape, lambda n, g: (0,) * value.ndim)


def self_forward(blocks, own, query, rel, own_key, own_value, keys, values, index):
    streams, seqs, rows, width = query.shape
    seq = keys.shape[1]
    slots = rows // BLK
    total = 2 * streams * BLK
    return pl.pallas_call(
        self_forward_kernel,
        grid=(seqs, width // 256),
        in_specs=[
            smem_spec(),
            smem_spec(),
            group_spec(streams, rows, 256),
            group_spec(streams, rows, 128),
            group_spec(streams - 1, rows, 256),
            group_spec(streams - 1, rows, 256),
            full_spec(seq, 256),
            full_spec(seq, 256),
            whole_spec(index),
        ],
        out_specs=[
            group_spec(streams, rows, 256),
            prob_spec(slots, total, seq),
            prob_spec(slots, total, 128),
        ],
        out_shape=[
            jax.ShapeDtypeStruct(query.shape, BF16),
            jax.ShapeDtypeStruct((seqs, width // 128, slots, total, seq), BF16),
            jax.ShapeDtypeStruct((seqs, width // 128, slots, total, 128), BF16),
        ],
        compiler_params=pltpu.CompilerParams(vmem_limit_bytes=LIMIT),
        cost_estimate=estimate(40e9, 80e6),
        name="self_forward",
    )(blocks, own, query, rel, own_key, own_value, keys, values, index)


def self_backward(
    blocks, own, query, own_key, own_value, keys, values, hot, mixed, grad, probs, own_probs
):
    streams, seqs, rows, width = query.shape
    seq = keys.shape[1]
    slots = rows // BLK
    total = 2 * streams * BLK
    return pl.pallas_call(
        self_backward_kernel,
        grid=(seqs, width // 256),
        in_specs=[
            smem_spec(),
            smem_spec(),
            group_spec(streams, rows, 256),
            group_spec(streams - 1, rows, 256),
            group_spec(streams - 1, rows, 256),
            full_spec(seq, 256),
            full_spec(seq, 256),
            whole_spec(hot),
            group_spec(streams, rows, 256),
            group_spec(streams, rows, 256),
            prob_spec(slots, total, seq),
            prob_spec(slots, total, 128),
        ],
        out_specs=[
            group_spec(streams, rows, 256),
            group_spec(streams, rows, 128),
            group_spec(streams - 1, rows, 256),
            group_spec(streams - 1, rows, 256),
            full_spec(seq, 256),
            full_spec(seq, 256),
        ],
        out_shape=[
            jax.ShapeDtypeStruct(query.shape, BF16),
            jax.ShapeDtypeStruct((streams, seqs, rows, width // 2), BF16),
            jax.ShapeDtypeStruct(own_key.shape, BF16),
            jax.ShapeDtypeStruct(own_key.shape, BF16),
            jax.ShapeDtypeStruct(keys.shape, BF16),
            jax.ShapeDtypeStruct(keys.shape, BF16),
        ],
        scratch_shapes=[pltpu.VMEM((seq, 256), F32), pltpu.VMEM((seq, 256), F32)],
        compiler_params=pltpu.CompilerParams(vmem_limit_bytes=LIMIT),
        cost_estimate=estimate(90e9, 100e6),
        name="self_backward",
    )(blocks, own, query, own_key, own_value, keys, values, hot, mixed, grad, probs, own_probs)


def cross_forward_kernel(query_ref, key_ref, value_ref, out_ref, prob_ref):
    rows = query_ref.shape[2]
    low = low_lanes(rows)
    for pair in range(2):
        lanes = slice(128 * pair, 128 * pair + 128)
        pairs = pair_rows(query_ref[0, 0, :, lanes], low) * jnp.asarray(SCALE, BF16)
        scores = dot_nt(pairs, key_ref[0, :, lanes])
        top = jnp.max(scores, axis=1, keepdims=True)
        weights = jnp.exp(scores - top)
        inverse = 1.0 / jnp.sum(weights, axis=1, keepdims=True)
        probs = (weights * inverse).astype(BF16)
        prob_ref[0, 0, pair] = probs
        mixed = dot_nn(probs, value_ref[0, :, lanes])
        out_ref[0, 0, :, lanes] = jnp.where(low, mixed[:rows], mixed[rows:]).astype(BF16)


def cross_backward_kernel(
    query_ref,
    key_ref,
    value_ref,
    out_ref,
    grad_ref,
    prob_ref,
    grad_query_ref,
    grad_key_ref,
    grad_value_ref,
    key_total,
    value_total,
):
    rows = query_ref.shape[2]
    low = low_lanes(rows)
    stream = pl.program_id(2)

    @pl.when(stream == 0)
    def _():
        key_total[...] = jnp.zeros_like(key_total)
        value_total[...] = jnp.zeros_like(value_total)

    for pair in range(2):
        lanes = slice(128 * pair, 128 * pair + 128)
        pairs = pair_rows(query_ref[0, 0, :, lanes], low) * jnp.asarray(SCALE, BF16)
        keys = key_ref[0, :, lanes]
        grads = pair_rows(grad_ref[0, 0, :, lanes], low)
        mixed = out_ref[0, 0, :, lanes].astype(F32)
        delta = jnp.sum(
            grads.astype(F32) * jnp.concatenate([mixed, mixed], axis=0), axis=1, keepdims=True
        )
        probs = prob_ref[0, 0, pair]
        grad_probs = dot_nt(grads, value_ref[0, :, lanes])
        grad_scores = (probs.astype(F32) * (grad_probs - delta)).astype(BF16)
        value_total[:, lanes] += dot_tn(probs, grads)
        key_total[:, lanes] += dot_tn(grad_scores, pairs)
        moved = dot_nn(grad_scores, keys) * SCALE
        grad_query_ref[0, 0, :, lanes] = jnp.where(low, moved[:rows], moved[rows:]).astype(BF16)

    @pl.when(stream == pl.num_programs(2) - 1)
    def _():
        grad_key_ref[0] = key_total[...].astype(BF16)
        grad_value_ref[0] = value_total[...].astype(BF16)


def stream_spec(rows):
    return pl.BlockSpec((1, 1, rows, 256), lambda n, g, s: (s, n, 0, g))


def memory_spec(rows):
    return pl.BlockSpec((1, rows, 256), lambda n, g, s: (n, 0, g))


def cross_prob_spec(rows, memory):
    return pl.BlockSpec((1, 1, 2, 2 * rows, memory), lambda n, g, s: (s, n, g, 0, 0))


def cross_forward(query, keys, values):
    streams, seqs, rows, width = query.shape
    memory = keys.shape[1]
    return pl.pallas_call(
        cross_forward_kernel,
        grid=(seqs, width // 256, streams),
        in_specs=[stream_spec(rows), memory_spec(memory), memory_spec(memory)],
        out_specs=[stream_spec(rows), cross_prob_spec(rows, memory)],
        out_shape=[
            jax.ShapeDtypeStruct(query.shape, BF16),
            jax.ShapeDtypeStruct((streams, seqs, width // 128, 2 * rows, memory), BF16),
        ],
        compiler_params=pltpu.CompilerParams(vmem_limit_bytes=LIMIT),
        cost_estimate=estimate(26e9, 20e6),
        name="cross_forward",
    )(query, keys, values)


def cross_backward(query, keys, values, mixed, grad, probs):
    streams, seqs, rows, width = query.shape
    memory = keys.shape[1]
    return pl.pallas_call(
        cross_backward_kernel,
        grid=(seqs, width // 256, streams),
        in_specs=[
            stream_spec(rows),
            memory_spec(memory),
            memory_spec(memory),
            stream_spec(rows),
            stream_spec(rows),
            cross_prob_spec(rows, memory),
        ],
        out_specs=[stream_spec(rows), memory_spec(memory), memory_spec(memory)],
        out_shape=[
            jax.ShapeDtypeStruct(query.shape, BF16),
            jax.ShapeDtypeStruct(keys.shape, BF16),
            jax.ShapeDtypeStruct(keys.shape, BF16),
        ],
        scratch_shapes=[pltpu.VMEM((memory, 256), F32), pltpu.VMEM((memory, 256), F32)],
        compiler_params=pltpu.CompilerParams(vmem_limit_bytes=LIMIT),
        cost_estimate=estimate(60e9, 30e6),
        name="cross_backward",
    )(query, keys, values, mixed, grad, probs)


def bucket_index(own_blocks, bucket_table, seq):
    span = bucket_table.shape[0]
    front = seq - BLK
    length = 2 * seq + BLK
    line = jnp.zeros((length,), jnp.int32).at[front : front + span].set(bucket_table)
    flat = jnp.tile(line, BLK + 1)[: BLK * (length + 1)]
    skew = flat.reshape(BLK, length + 1)
    parts = [
        lax.dynamic_slice_in_dim(skew, own_blocks[slot] * BLK, seq, axis=1)
        for slot in range(own_blocks.shape[0])
    ]
    return jnp.concatenate(parts, axis=0)


def bucket_hots(bucket_table, seq, front):
    span = bucket_table.shape[0]
    depth = CHUNK + seq + 128
    line = jnp.full((front + span + depth,), -1, jnp.int32)
    line = line.at[front : front + span].set(bucket_table)[:depth]
    lane = jnp.arange(128, dtype=jnp.int32)
    return (line[:, None] == lane[None, :]).astype(BF16)


EPSILON = 1e-05
FULL = ("fsdp", "ctx")


def gather(shard, ranks):
    rows = shard.shape[0] // ranks
    piece = lax.dynamic_slice_in_dim(shard, lax.axis_index("ctx") * rows, rows)
    return lax.all_gather(piece, FULL, axis=0, tiled=True)


def reduce_rows(grad):
    piece = lax.psum_scatter(grad.astype(BF16), FULL, scatter_dimension=0, tiled=True)
    return lax.all_gather(piece, "ctx", axis=0, tiled=True).astype(F32)


def flat(value):
    return value.reshape(-1, value.shape[-1])


def normalize(values):
    average = jnp.mean(values, axis=-1, keepdims=True)
    centred = values - average
    variance = jnp.mean(centred * centred, axis=-1, keepdims=True)
    rate = lax.rsqrt(variance + EPSILON)
    return centred * rate, rate


def norm_back(grad, normal, rate, gain):
    inner = grad * gain
    first = jnp.mean(inner, axis=-1, keepdims=True)
    second = jnp.mean(inner * normal, axis=-1, keepdims=True)
    back = (inner - first - normal * second) * rate
    return back, jnp.sum(grad * normal, axis=0), jnp.sum(grad, axis=0)


def gelu_parts(inner):
    share = 0.5 * (1.0 + lax.erf(inner * (0.5**0.5)))
    slope = share + inner * jnp.exp(-0.5 * inner * inner) * ((0.5 / jnp.pi) ** 0.5)
    return (inner * share).astype(BF16), slope.astype(BF16)


def head_major(weight):
    rows, width = weight.shape
    return weight.reshape(rows, BUCKETS, width // BUCKETS).transpose(0, 2, 1).reshape(rows, width)


def bucket_major(weight):
    rows, width = weight.shape
    return weight.reshape(rows, width // BUCKETS, BUCKETS).transpose(0, 2, 1).reshape(rows, width)


def body(
    ranks,
    hidden,
    encoded,
    assign,
    bucket_table,
    w_query,
    w_key,
    w_value,
    w_rel,
    w_out,
    gain_one,
    shift_one,
    c_query,
    c_key,
    c_value,
    c_out,
    gain_two,
    shift_two,
    w_inner,
    w_outer,
    gain_three,
    shift_three,
    cotangent,
):
    seqs, rows, streams, width = hidden.shape
    seq = rows * ranks
    rank = lax.axis_index("ctx")
    slots = rows // BLK
    own_blocks = lax.dynamic_slice_in_dim(assign, rank * slots, slots)
    own = bucket_table[BLK - 1 : BLK]
    index = bucket_index(own_blocks, bucket_table, seq)
    hot = bucket_hots(bucket_table, seq, CHUNK)
    places = (assign[:, None] * BLK + jnp.arange(BLK, dtype=jnp.int32)[None, :]).reshape(-1)
    order = (places[None, :] == (seq - 1 - jnp.arange(seq, dtype=jnp.int32))[:, None]).astype(BF16)

    full_main = gather(jnp.concatenate([w_query, head_major(w_rel), w_key, w_value], axis=1), ranks)
    cut = w_query.shape[1] + w_rel.shape[1]
    w_query, w_rel = full_main[:, :width], full_main[:, width:cut]
    w_key, w_value = full_main[:, cut : cut + width], full_main[:, cut + width :]
    norms = jnp.stack([gain_one, shift_one, gain_two, shift_two, gain_three, shift_three])
    norms = lax.all_gather(norms, "fsdp", axis=1, tiled=True).astype(F32)
    gain_one, shift_one, gain_two, shift_two, gain_three, shift_three = (
        norms[place : place + 1] for place in range(6)
    )
    main = lax.all_gather(hidden[:, :, 0, :], "ctx", axis=1, tiled=True)
    memory = lax.all_gather(encoded, "ctx", axis=1, tiled=True)
    w_out = gather(w_out, ranks)
    full_cross = gather(jnp.concatenate([c_key, c_value], axis=1), ranks)
    c_key, c_value = full_cross[:, :width], full_cross[:, width:]
    c_query = gather(c_query, ranks)
    c_out = gather(c_out, ranks)
    w_inner = gather(w_inner, ranks)
    w_outer = gather(w_outer, ranks)

    stacked = jnp.transpose(hidden, (2, 0, 1, 3))
    shape = stacked.shape
    lines = flat(stacked)
    own_shape = (streams - 1,) + shape[1:]
    own_lines = flat(stacked[1:])
    main = jnp.einsum("mu,nud->nmd", order, main, preferred_element_type=F32).astype(BF16)
    main_lines = flat(main)
    main_shape = main.shape
    query = dot_nn(lines, w_query).astype(BF16).reshape(shape)
    rel = dot_nn(lines, w_rel).astype(BF16).reshape(shape[:-1] + (-1,))
    own_keys = dot_nn(own_lines, w_key).astype(BF16).reshape(own_shape)
    own_values = dot_nn(own_lines, w_value).astype(BF16).reshape(own_shape)
    keys = dot_nn(main_lines, w_key).astype(BF16).reshape(main_shape)
    values = dot_nn(main_lines, w_value).astype(BF16).reshape(main_shape)
    mixed, probs, own_probs = self_forward(
        own_blocks, own, query, rel, own_keys, own_values, keys, values, index
    )
    normal_one, rate_one = normalize(lines.astype(F32) + dot_nn(flat(mixed), w_out))
    h_one = normal_one * gain_one + shift_one
    h_one_low = h_one.astype(BF16)
    cross_query = dot_nn(h_one_low, c_query).astype(BF16).reshape(shape)
    memory_lines = flat(memory)
    cross_keys = dot_nn(memory_lines, c_key).astype(BF16).reshape(memory.shape)
    cross_values = dot_nn(memory_lines, c_value).astype(BF16).reshape(memory.shape)
    cross_mixed, cross_probs = cross_forward(cross_query, cross_keys, cross_values)
    normal_two, rate_two = normalize(h_one + dot_nn(flat(cross_mixed), c_out))
    h_two = normal_two * gain_two + shift_two
    h_two_low = h_two.astype(BF16)
    active, slope = gelu_parts(dot_nn(h_two_low, w_inner))
    normal_three, rate_three = normalize(h_two + dot_nn(active, w_outer))
    output = (normal_three * gain_three + shift_three).astype(BF16)
    output = jnp.transpose(output.reshape(shape), (1, 2, 0, 3))

    grad = flat(jnp.transpose(cotangent, (2, 0, 1, 3))).astype(F32)
    grad_three, gain_three, shift_three = norm_back(grad, normal_three, rate_three, gain_three)
    grad_low = grad_three.astype(BF16)
    w_outer_grad = reduce_rows(dot_tn(active, grad_low))
    grad_inner = (dot_nt(grad_low, w_outer) * slope.astype(F32)).astype(BF16)
    w_inner_grad = reduce_rows(dot_tn(h_two_low, grad_inner))
    grad_h_two = grad_three + dot_nt(grad_inner, w_inner)
    grad_two, gain_two, shift_two = norm_back(grad_h_two, normal_two, rate_two, gain_two)
    grad_low = grad_two.astype(BF16)
    c_out_grad = reduce_rows(dot_tn(flat(cross_mixed), grad_low))
    grad_mixed = dot_nt(grad_low, c_out).astype(BF16).reshape(shape)
    cross_query_grad, key_grad, value_grad = cross_backward(
        cross_query, cross_keys, cross_values, cross_mixed, grad_mixed, cross_probs
    )
    cross_query_grad = flat(cross_query_grad)
    key_grad, value_grad = flat(key_grad), flat(value_grad)
    c_query_grad = reduce_rows(dot_tn(h_one_low, cross_query_grad))
    grad_h_one = grad_two + dot_nt(cross_query_grad, c_query)
    grad_one, gain_one, shift_one = norm_back(grad_h_one, normal_one, rate_one, gain_one)
    grad_low = grad_one.astype(BF16)
    w_out_grad = reduce_rows(dot_tn(flat(mixed), grad_low))
    grad_mixed = dot_nt(grad_low, w_out).astype(BF16).reshape(shape)
    cross_grad = reduce_rows(
        jnp.concatenate([dot_tn(memory_lines, key_grad), dot_tn(memory_lines, value_grad)], axis=1)
    )
    encoded_grad = (dot_nt(key_grad, c_key) + dot_nt(value_grad, c_value)).astype(BF16)
    encoded_grad = lax.psum_scatter(
        encoded_grad.reshape(memory.shape), "ctx", scatter_dimension=1, tiled=True
    ).astype(F32)
    query_grad, rel_grad, own_key_grad, own_value_grad, key_grad, value_grad = self_backward(
        own_blocks,
        own,
        query,
        own_keys,
        own_values,
        keys,
        values,
        hot,
        mixed,
        grad_mixed,
        probs,
        own_probs,
    )
    query_grad, rel_grad = flat(query_grad), flat(rel_grad)
    own_key_grad, own_value_grad = flat(own_key_grad), flat(own_value_grad)
    key_grad, value_grad = flat(key_grad), flat(value_grad)
    main_grad = (dot_nt(key_grad, w_key) + dot_nt(value_grad, w_value)).astype(BF16)
    main_grad = jnp.einsum(
        "mu,nmd->nud", order, main_grad.reshape(main_shape), preferred_element_type=F32
    ).astype(BF16)
    main_grad = lax.psum_scatter(main_grad, "ctx", scatter_dimension=1, tiled=True).astype(F32)
    full_grad = reduce_rows(
        jnp.concatenate(
            [
                dot_tn(lines, query_grad),
                dot_tn(lines, rel_grad),
                dot_tn(own_lines, own_key_grad) + dot_tn(main_lines, key_grad),
                dot_tn(own_lines, own_value_grad) + dot_tn(main_lines, value_grad),
            ],
            axis=1,
        )
    )
    own_grad = dot_nt(own_key_grad, w_key) + dot_nt(own_value_grad, w_value)
    grad_lines = grad_one + dot_nt(query_grad, w_query) + dot_nt(rel_grad, w_rel)
    grad_lines = grad_lines.reshape(shape) + jnp.concatenate(
        [main_grad[None], own_grad.reshape(own_shape)], axis=0
    )
    grad_hidden = jnp.transpose(grad_lines, (1, 2, 0, 3))
    norms = jnp.stack([gain_one, shift_one, gain_two, shift_two, gain_three, shift_three])
    norms = lax.psum_scatter(lax.psum(norms, "ctx"), "fsdp", scatter_dimension=1, tiled=True)
    gain_one, shift_one, gain_two, shift_two, gain_three, shift_three = (
        norms[place] for place in range(6)
    )
    return (
        output,
        grad_hidden,
        encoded_grad,
        full_grad[:, :width],
        full_grad[:, cut : cut + width],
        full_grad[:, cut + width :],
        bucket_major(full_grad[:, width:cut]),
        w_out_grad,
        gain_one,
        shift_one,
        c_query_grad,
        cross_grad[:, :width],
        cross_grad[:, width:],
        c_out_grad,
        gain_two,
        shift_two,
        w_inner_grad,
        w_outer_grad,
        gain_three,
        shift_three,
    )


def solution(mesh):
    matrix, vector = P("fsdp", None), P("fsdp")
    rows = P("fsdp", "ctx", None, None)
    weights = (matrix,) * 5 + (vector,) * 2 + (matrix,) * 4 + (vector,) * 2 + (matrix,) * 2
    weights = weights + (vector,) * 2
    in_specs = (rows, P("fsdp", "ctx", None), P(), P()) + weights + (rows,)
    out_specs = (rows, rows, P("fsdp", "ctx", None)) + weights
    return jax.shard_map(
        functools.partial(body, mesh.shape["ctx"]),
        mesh=mesh,
        in_specs=in_specs,
        out_specs=out_specs,
        check_vma=False,
    )
```

```python
import functools
import jax
import jax.numpy as jnp
from jax import lax
from jax.sharding import PartitionSpec as P
from jax.experimental import pallas as pl
from jax.experimental.pallas import tpu as pltpu

HEAD_DIM = 64
BUCKETS = 32
BLK = 32
CHUNK = 256
FILLER = -1e30
SCALE = HEAD_DIM ** (-0.5)
LIMIT = 60 * 1024 * 1024
F32 = jnp.float32
BF16 = jnp.bfloat16


def dot_nt(left, right):
    return lax.dot_general(left, right, (((1,), (1,)), ((), ())), preferred_element_type=F32)


def dot_tn(left, right):
    return lax.dot_general(left, right, (((0,), (0,)), ((), ())), preferred_element_type=F32)


def dot_nn(left, right):
    return jnp.dot(left, right, preferred_element_type=F32)


def low_lanes(rows):
    return lax.broadcasted_iota(jnp.int32, (rows, 128), 1) < HEAD_DIM


def pair_rows(value, low):
    zero = jnp.zeros_like(value)
    return jnp.concatenate([jnp.where(low, value, zero), jnp.where(low, zero, value)], axis=0)


def self_parts(place, query_ref, own_key_ref, own_value_ref):
    slot, pair = place // 2, place % 2
    rows = pl.ds(pl.multiple_of(slot * BLK, BLK), BLK)
    lanes = pl.ds(pl.multiple_of(pair * 128, 128), 128)
    total = query_ref.shape[0] * BLK
    low = low_lanes(total)
    query = query_ref[:, 0, rows, lanes].reshape(total, 128)
    pairs = pair_rows(query, low) * jnp.asarray(SCALE, BF16)
    zero = jnp.zeros((BLK, 128), F32)
    own_key = own_key_ref[:, 0, rows, lanes].reshape(total - BLK, 128).astype(F32)
    own_key = jnp.concatenate([zero, own_key], axis=0)
    own_value = own_value_ref[:, 0, rows, lanes].reshape(total - BLK, 128).astype(F32)
    own_value = jnp.concatenate([zero, own_value], axis=0)
    return slot, pair, rows, lanes, low, pairs, own_key, own_value


def self_forward_kernel(
    blocks,
    own_ref,
    query_ref,
    rel_ref,
    own_key_ref,
    own_value_ref,
    key_ref,
    value_ref,
    index_ref,
    out_ref,
    prob_ref,
    own_prob_ref,
):
    seq = key_ref.shape[1]
    streams = query_ref.shape[0]
    total = streams * BLK

    def step(place, carry):
        slot, pair, rows, lanes, low, pairs, own_key, own_value = self_parts(
            place, query_ref, own_key_ref, own_value_ref
        )
        block = blocks[slot]
        rel = rel_ref[:, 0, rows, :].reshape(total, 128).astype(F32)
        table = jnp.concatenate(
            [pltpu.roll(rel, pair * 64, 1), pltpu.roll(rel, pair * 64 + 96, 1)], axis=0
        )
        lane = lax.broadcasted_iota(jnp.int32, (2 * total, 128), 1)
        own = jnp.where(lane == own_ref[0], table, 0.0)
        own = own + pairs.astype(F32) * jnp.concatenate([own_key, own_key], axis=0)
        own = jnp.sum(own, axis=1, keepdims=True)
        row = lax.broadcasted_iota(jnp.int32, (2 * total, 1), 0)
        main = jnp.logical_or(row < BLK, jnp.logical_and(row >= total, row < total + BLK))
        own = jnp.where(main, FILLER, own)
        count = (block * BLK) // CHUNK + 1
        for parts in range(1, seq // CHUNK + 1):
            width = parts * CHUNK

            @pl.when(count == parts)
            def _():
                span = slice(seq - width, seq)
                index = index_ref[rows, span]
                bias = [
                    jnp.take_along_axis(
                        table,
                        jnp.concatenate([index[:, start : start + 128]] * (2 * streams), axis=0),
                        axis=1,
                    )
                    for start in range(0, width, 128)
                ]
                scores = dot_nt(pairs, key_ref[0, span, lanes]) + jnp.concatenate(bias, axis=1)
                column = lax.broadcasted_iota(jnp.int32, (2 * total, CHUNK), 1)
                seen = column >= width - BLK * (block + 1)
                first = jnp.where(seen, scores[:, :CHUNK], FILLER)
                scores = (
                    jnp.concatenate([first, scores[:, CHUNK:]], axis=1) if parts > 1 else first
                )
                top = jnp.maximum(jnp.max(scores, axis=1, keepdims=True), own)
                weights = jnp.exp(scores - top)
                own_weight = jnp.exp(own - top)
                inverse = 1.0 / (jnp.sum(weights, axis=1, keepdims=True) + own_weight)
                probs = (weights * inverse).astype(BF16)
                prob_ref[0, pair, slot, :, span] = probs
                own_prob = own_weight * inverse
                own_prob_ref[0, pair, slot] = jnp.broadcast_to(own_prob, (2 * total, 128)).astype(
                    BF16
                )
                mixed = dot_nn(probs, value_ref[0, span, lanes])
                result = jnp.where(
                    low,
                    mixed[:total] + own_prob[:total] * own_value,
                    mixed[total:] + own_prob[total:] * own_value,
                )
                out_ref[:, 0, rows, lanes] = result.astype(BF16).reshape(streams, BLK, 128)

        return carry

    lax.fori_loop(0, 2 * blocks.shape[0], step, 0)


def self_backward_kernel(
    group,
    blocks,
    own_ref,
    query_ref,
    own_key_ref,
    own_value_ref,
    key_ref,
    value_ref,
    hot_ref,
    out_ref,
    grad_ref,
    prob_ref,
    own_prob_ref,
    grad_query_ref,
    grad_rel_ref,
    grad_own_key_ref,
    grad_own_value_ref,
    grad_key_ref,
    grad_value_ref,
    key_total,
    value_total,
):
    seq = key_ref.shape[1]
    streams = query_ref.shape[0]
    total = streams * BLK
    key_total[...] = jnp.zeros_like(key_total)
    value_total[...] = jnp.zeros_like(value_total)

    def step(place, carry):
        slot, pair, rows, lanes, low, pairs, own_key, own_value = self_parts(
            place, query_ref, own_key_ref, own_value_ref
        )
        block = blocks[slot]
        grads = pair_rows(grad_ref[:, 0, rows, lanes].reshape(total, 128), low)
        wide = grads.astype(F32)
        mixed = out_ref[:, 0, rows, lanes].reshape(total, 128).astype(F32)
        delta = jnp.sum(wide * jnp.concatenate([mixed, mixed], axis=0), axis=1, keepdims=True)
        grad_own = jnp.sum(
            wide * jnp.concatenate([own_value, own_value], axis=0), axis=1, keepdims=True
        )
        own_prob = own_prob_ref[0, pair, slot].astype(F32)
        grad_own = own_prob * (grad_own - delta)
        part = grad_own * pairs.astype(F32)
        part = (part[:total] + part[total:])[BLK:]
        grad_own_key_ref[:, 0, rows, lanes] = part.astype(BF16).reshape(streams - 1, BLK, 128)
        part = own_prob * wide
        part = (part[:total] + part[total:])[BLK:]
        grad_own_value_ref[:, 0, rows, lanes] = part.astype(BF16).reshape(streams - 1, BLK, 128)
        count = (block * BLK) // CHUNK + 1
        for parts in range(1, seq // CHUNK + 1):
            width = parts * CHUNK

            @pl.when(count == parts)
            def _():
                span = slice(seq - width, seq)
                probs = prob_ref[0, pair, slot, :, span]
                grad_probs = dot_nt(grads, value_ref[0, span, lanes])
                grad_scores = probs.astype(F32) * (grad_probs - delta)
                low_scores = grad_scores.astype(BF16)
                value_total[span, lanes] += dot_tn(probs, grads)
                key_total[span, lanes] += dot_tn(low_scores, pairs)
                moved = dot_nn(low_scores, key_ref[0, span, lanes])
                moved = jnp.where(
                    low,
                    moved[:total] + grad_own[:total] * own_key,
                    moved[total:] + grad_own[total:] * own_key,
                )
                grad_query_ref[:, 0, rows, lanes] = (
                    (moved * SCALE).astype(BF16).reshape(streams, BLK, 128)
                )
                pad = jnp.zeros((BLK, 128), F32)
                skewed = []
                for start in range(0, 2 * total, BLK):
                    piece = jnp.concatenate([grad_scores[start : start + BLK], pad], axis=1)
                    skewed.append(pltpu.roll(piece, 0, 1, stride=1, stride_axis=0).astype(BF16))
                begin = pl.multiple_of(BLK * (block + 1) - width + CHUNK, BLK)
                hots = hot_ref[pl.ds(begin, width + 128), :]
                sums = dot_nn(jnp.concatenate(skewed, axis=0), hots)
                lane = lax.broadcasted_iota(jnp.int32, (2 * total, 128), 1)
                sums = sums + jnp.where(lane == own_ref[0], grad_own, 0.0)
                sums = pltpu.roll(sums[:total], pair * 64, 1) + pltpu.roll(
                    sums[total:], pair * 64 + BUCKETS, 1
                )
                lane = lax.broadcasted_iota(jnp.int32, (total, 128), 1)
                mine = jnp.logical_and(lane >= 64 * pair, lane < 64 * pair + 64)
                before = grad_rel_ref[:, 0, rows, :].reshape(total, 128)
                sums = jnp.where(mine, sums.astype(BF16), before)
                grad_rel_ref[:, 0, rows, :] = sums.reshape(streams, BLK, 128)

        return carry

    lax.fori_loop(0, 2 * blocks.shape[0], step, 0)
    grad_key_ref[0] = key_total[...].astype(BF16)
    grad_value_ref[0] = value_total[...].astype(BF16)


def group_spec(streams, rows, lanes):
    return pl.BlockSpec((streams, 1, rows, lanes), lambda n, g: (0, n, 0, g))


def full_spec(rows, lanes):
    return pl.BlockSpec((1, rows, lanes), lambda n, g: (n, 0, g))


def smem_spec():
    return pl.BlockSpec(memory_space=pltpu.SMEM)


def estimate(flops, moved):
    return pl.CostEstimate(flops=int(flops), bytes_accessed=int(moved), transcendentals=0)


def prob_spec(slots, total, width):
    return pl.BlockSpec((1, 2, slots, total, width), lambda n, g: (n, g, 0, 0, 0))


def whole_spec(value):
    return pl.BlockSpec(value.shape, lambda n, g: (0,) * value.ndim)


def self_forward(blocks, own, query, rel, own_key, own_value, keys, values, index):
    streams, seqs, rows, width = query.shape
    seq = keys.shape[1]
    slots = rows // BLK
    total = 2 * streams * BLK
    return pl.pallas_call(
        self_forward_kernel,
        grid=(seqs, width // 256),
        in_specs=[
            smem_spec(),
            smem_spec(),
            group_spec(streams, rows, 256),
            group_spec(streams, rows, 128),
            group_spec(streams - 1, rows, 256),
            group_spec(streams - 1, rows, 256),
            full_spec(seq, 256),
            full_spec(seq, 256),
            whole_spec(index),
        ],
        out_specs=[
            group_spec(streams, rows, 256),
            prob_spec(slots, total, seq),
            prob_spec(slots, total, 128),
        ],
        out_shape=[
            jax.ShapeDtypeStruct(query.shape, BF16),
            jax.ShapeDtypeStruct((seqs, width // 128, slots, total, seq), BF16),
            jax.ShapeDtypeStruct((seqs, width // 128, slots, total, 128), BF16),
        ],
        compiler_params=pltpu.CompilerParams(vmem_limit_bytes=LIMIT),
        cost_estimate=estimate(150e9, 80e6),
        name="self_forward",
    )(blocks, own, query, rel, own_key, own_value, keys, values, index)


def self_backward(
    group, blocks, own, query, own_key, own_value, keys, values, hot, mixed, grad, probs, own_probs
):
    streams, seqs, rows, width = query.shape
    seq = keys.shape[1]
    slots = rows // BLK
    total = 2 * streams * BLK

    def lines(count):
        return pl.BlockSpec((count, 1, rows, 256), lambda n, g, b, o: (0, n, 0, g[0]))

    def result(count, lanes):
        return pl.BlockSpec((count, 1, rows, lanes), lambda n, g, b, o: (0, n, 0, 0))

    def shape(count, lanes):
        return jax.ShapeDtypeStruct((count, seqs, rows, lanes), BF16)

    def stored(lanes):
        return pl.BlockSpec((1, 2, slots, total, lanes), lambda n, g, b, o: (n, g[0], 0, 0, 0))

    memory = pl.BlockSpec((1, seq, 256), lambda n, g, b, o: (n, 0, g[0]))
    memory_result = pl.BlockSpec((1, seq, 256), lambda n, g, b, o: (n, 0, 0))
    memory_shape = jax.ShapeDtypeStruct((seqs, seq, 256), BF16)
    return pl.pallas_call(
        self_backward_kernel,
        grid_spec=pltpu.PrefetchScalarGridSpec(
            num_scalar_prefetch=3,
            grid=(seqs,),
            in_specs=[
                lines(streams),
                lines(streams - 1),
                lines(streams - 1),
                memory,
                memory,
                pl.BlockSpec(hot.shape, lambda n, g, b, o: (0, 0)),
                lines(streams),
                lines(streams),
                stored(seq),
                stored(128),
            ],
            out_specs=[
                result(streams, 256),
                result(streams, 128),
                result(streams - 1, 256),
                result(streams - 1, 256),
                memory_result,
                memory_result,
            ],
            scratch_shapes=[pltpu.VMEM((seq, 256), F32), pltpu.VMEM((seq, 256), F32)],
        ),
        out_shape=[
            shape(streams, 256),
            shape(streams, 128),
            shape(streams - 1, 256),
            shape(streams - 1, 256),
            memory_shape,
            memory_shape,
        ],
        compiler_params=pltpu.CompilerParams(vmem_limit_bytes=LIMIT),
        cost_estimate=estimate(145e9 / 4, 100e6 / 4),
        name="self_backward",
    )(group, blocks, own, query, own_key, own_value, keys, values, hot, mixed, grad, probs, own_probs)


def cross_forward_kernel(query_ref, key_ref, value_ref, out_ref, prob_ref):
    rows = query_ref.shape[2]
    low = low_lanes(rows)
    for pair in range(2):
        lanes = slice(128 * pair, 128 * pair + 128)
        pairs = pair_rows(query_ref[0, 0, :, lanes], low) * jnp.asarray(SCALE, BF16)
        scores = dot_nt(pairs, key_ref[0, :, lanes])
        top = jnp.max(scores, axis=1, keepdims=True)
        weights = jnp.exp(scores - top)
        inverse = 1.0 / jnp.sum(weights, axis=1, keepdims=True)
        probs = (weights * inverse).astype(BF16)
        prob_ref[0, 0, pair] = probs
        mixed = dot_nn(probs, value_ref[0, :, lanes])
        out_ref[0, 0, :, lanes] = jnp.where(low, mixed[:rows], mixed[rows:]).astype(BF16)


def cross_backward_kernel(
    query_ref,
    key_ref,
    value_ref,
    out_ref,
    grad_ref,
    prob_ref,
    grad_query_ref,
    grad_key_ref,
    grad_value_ref,
    key_total,
    value_total,
):
    rows = query_ref.shape[2]
    low = low_lanes(rows)
    stream = pl.program_id(2)

    @pl.when(stream == 0)
    def _():
        key_total[...] = jnp.zeros_like(key_total)
        value_total[...] = jnp.zeros_like(value_total)

    for pair in range(2):
        lanes = slice(128 * pair, 128 * pair + 128)
        pairs = pair_rows(query_ref[0, 0, :, lanes], low) * jnp.asarray(SCALE, BF16)
        keys = key_ref[0, :, lanes]
        grads = pair_rows(grad_ref[0, 0, :, lanes], low)
        mixed = out_ref[0, 0, :, lanes].astype(F32)
        delta = jnp.sum(
            grads.astype(F32) * jnp.concatenate([mixed, mixed], axis=0), axis=1, keepdims=True
        )
        probs = prob_ref[0, 0, pair]
        grad_probs = dot_nt(grads, value_ref[0, :, lanes])
        grad_scores = (probs.astype(F32) * (grad_probs - delta)).astype(BF16)
        value_total[:, lanes] += dot_tn(probs, grads)
        key_total[:, lanes] += dot_tn(grad_scores, pairs)
        moved = dot_nn(grad_scores, keys) * SCALE
        grad_query_ref[0, 0, :, lanes] = jnp.where(low, moved[:rows], moved[rows:]).astype(BF16)

    @pl.when(stream == pl.num_programs(2) - 1)
    def _():
        grad_key_ref[0] = key_total[...].astype(BF16)
        grad_value_ref[0] = value_total[...].astype(BF16)


def stream_spec(rows):
    return pl.BlockSpec((1, 1, rows, 256), lambda n, g, s: (s, n, 0, g))


def memory_spec(rows):
    return pl.BlockSpec((1, rows, 256), lambda n, g, s: (n, 0, g))


def cross_prob_spec(rows, memory):
    return pl.BlockSpec((1, 1, 2, 2 * rows, memory), lambda n, g, s: (s, n, g, 0, 0))


def cross_forward(query, keys, values):
    streams, seqs, rows, width = query.shape
    memory = keys.shape[1]
    return pl.pallas_call(
        cross_forward_kernel,
        grid=(seqs, width // 256, streams),
        in_specs=[stream_spec(rows), memory_spec(memory), memory_spec(memory)],
        out_specs=[stream_spec(rows), cross_prob_spec(rows, memory)],
        out_shape=[
            jax.ShapeDtypeStruct(query.shape, BF16),
            jax.ShapeDtypeStruct((streams, seqs, width // 128, 2 * rows, memory), BF16),
        ],
        compiler_params=pltpu.CompilerParams(vmem_limit_bytes=LIMIT),
        cost_estimate=estimate(38e9, 40e6),
        name="cross_forward",
    )(query, keys, values)


def cross_backward(query, keys, values, mixed, grad, probs):
    streams, seqs, rows, width = query.shape
    memory = keys.shape[1]
    return pl.pallas_call(
        cross_backward_kernel,
        grid=(seqs, width // 256, streams),
        in_specs=[
            stream_spec(rows),
            memory_spec(memory),
            memory_spec(memory),
            stream_spec(rows),
            stream_spec(rows),
            cross_prob_spec(rows, memory),
        ],
        out_specs=[stream_spec(rows), memory_spec(memory), memory_spec(memory)],
        out_shape=[
            jax.ShapeDtypeStruct(query.shape, BF16),
            jax.ShapeDtypeStruct(keys.shape, BF16),
            jax.ShapeDtypeStruct(keys.shape, BF16),
        ],
        scratch_shapes=[pltpu.VMEM((memory, 256), F32), pltpu.VMEM((memory, 256), F32)],
        compiler_params=pltpu.CompilerParams(vmem_limit_bytes=LIMIT),
        cost_estimate=estimate(47e9, 50e6),
        name="cross_backward",
    )(query, keys, values, mixed, grad, probs)


def bucket_index(own_blocks, bucket_table, seq):
    span = bucket_table.shape[0]
    front = seq - BLK
    length = 2 * seq + BLK
    line = jnp.zeros((length,), jnp.int32).at[front : front + span].set(bucket_table)
    flat = jnp.tile(line, BLK + 1)[: BLK * (length + 1)]
    skew = flat.reshape(BLK, length + 1)
    parts = [
        lax.dynamic_slice_in_dim(skew, own_blocks[slot] * BLK, seq, axis=1)
        for slot in range(own_blocks.shape[0])
    ]
    return jnp.concatenate(parts, axis=0)


def bucket_hots(bucket_table, seq, front):
    span = bucket_table.shape[0]
    depth = CHUNK + seq + 128
    line = jnp.full((front + span + depth,), -1, jnp.int32)
    line = line.at[front : front + span].set(bucket_table)[:depth]
    lane = jnp.arange(128, dtype=jnp.int32)
    return (line[:, None] == lane[None, :]).astype(BF16)


EPSILON = 1e-05
FULL = ("fsdp", "ctx")


PARTNER = [(0, 1), (1, 0), (2, 3), (3, 2)]
ACROSS = [(0, 2), (2, 0), (1, 3), (3, 1)]


def gather(shard, ranks):
    rows = shard.shape[0] // ranks
    piece = lax.dynamic_slice_in_dim(shard, lax.axis_index("ctx") * rows, rows)
    return lax.all_gather(piece, FULL, axis=0, tiled=True)


def swap(value):
    return lax.ppermute(value, "ctx", PARTNER)


def pass_across(value):
    return lax.ppermute(value, "ctx", ACROSS)


def tie(*values):
    return lax.optimization_barrier(values)


def spread(piece):
    across = pass_across(piece)
    return piece, swap(piece), across, swap(across)


def place_kernel(rank, first, second, third, fourth, out_ref):
    for step, ref in enumerate((first, second, third, fourth)):

        @pl.when((rank[0] ^ step) == pl.program_id(0))
        def _():
            out_ref[:, 0] = ref[...]


def place(pieces):
    outer, rows, columns = pieces[0].shape
    return pl.pallas_call(
        place_kernel,
        grid=(4,),
        in_specs=[smem_spec()] + [whole_block(piece) for piece in pieces],
        out_specs=pl.BlockSpec((outer, 1, rows, columns), lambda step: (0, step, 0, 0)),
        out_shape=jax.ShapeDtypeStruct((outer, 4, rows, columns), pieces[0].dtype),
        compiler_params=pltpu.CompilerParams(vmem_limit_bytes=LIMIT),
        cost_estimate=estimate(0, 8 * pieces[0].size * 2),
        name="place",
    )(lax.axis_index("ctx").reshape(1), *pieces)


def whole_block(value):
    return pl.BlockSpec(
        value.shape, lambda step: (0,) * value.ndim, pipeline_mode=pl.Buffered(1)
    )


def gather_half(shard, ranks):
    if ranks != 4:
        return gather(shard, ranks)
    rows = shard.shape[0] // ranks
    piece = lax.dynamic_slice_in_dim(shard, lax.axis_index("ctx") * rows, rows)
    return lax.all_gather(piece, "fsdp", axis=0, tiled=False)


def gather_pass(piece, ranks):
    if ranks != 4:
        return (piece,)
    return piece, swap(piece), pass_across(piece)


def gather_rest(pieces, ranks):
    if ranks != 4:
        return pieces[0]
    piece, partner, across = pieces
    return place((piece, partner, across, swap(across))).reshape(-1, piece.shape[2])


def gather_rows(value, ranks):
    if ranks != 4:
        return lax.all_gather(value, "ctx", axis=1, tiled=True)
    return place(spread(value)).reshape(value.shape[0], -1, value.shape[2])


def column_part(count, *groups):
    def part(index, step):
        parts = []
        for group in groups:
            total = 0.0
            for left, right in group:
                columns = right.shape[1] // count
                right = lax.dynamic_slice_in_dim(right, index * columns, columns, axis=1)
                total = total + dot_tn(left, right)
            parts.append(total)
        return parts[0] if len(parts) == 1 else jnp.concatenate(parts, axis=1)

    return part


def block_part(count, value):
    rows = value.shape[1] // count

    def part(index, step):
        return lax.dynamic_slice_in_dim(value, index * rows, rows, axis=1).astype(F32)

    return part


class Exchange:
    def __init__(self, ranks, part):
        self.ranks = ranks
        self.part = part
        self.rank = lax.axis_index("ctx")

    def begin(self):
        if self.ranks != 4:
            every = [self.part(index, index).astype(BF16) for index in range(self.ranks)]
            self.values = (jnp.stack(every),)
            return
        corner = self.part(self.rank ^ 3, 3).astype(BF16)
        self.values = (corner, self.part(self.rank ^ 1, 1).astype(BF16))

    def turn(self):
        if self.ranks != 4:
            return
        corner, partner = (swap(value) for value in self.values)
        side = (self.part(self.rank ^ 2, 2) + corner.astype(F32)).astype(BF16)
        self.values = (side, partner)

    def fetch(self):
        if self.ranks == 4:
            side, partner = self.values
            self.values = (pass_across(side), partner)

    def end(self):
        if self.ranks != 4:
            mine = lax.psum_scatter(self.values[0], "ctx", scatter_dimension=0, tiled=True)
            return mine[0].astype(F32)
        side, partner = self.values
        return self.part(self.rank, 0) + partner.astype(F32) + side.astype(F32)


def hold(value, *items):
    packed = [item.values if isinstance(item, Exchange) else item for item in items]
    value, packed = tie(value, packed)
    for item, new in zip(items, packed):
        if isinstance(item, Exchange):
            item.values = new
    others = [new for item, new in zip(items, packed) if not isinstance(item, Exchange)]
    return (value, *others) if others else value


def scatter(total):
    return lax.psum_scatter(total.astype(BF16), "fsdp", scatter_dimension=0, tiled=True)


def collect(ranks, piece):
    if ranks != 4:
        whole = lax.all_gather(piece, "ctx", axis=0, tiled=False)
        return [whole[index].astype(F32) for index in range(ranks)]
    rank = lax.axis_index("ctx")
    pieces = spread(piece)
    ordered = []
    for index in range(4):
        chosen = pieces[3]
        for step in range(3):
            chosen = jnp.where((rank ^ step) == index, pieces[step], chosen)
        ordered.append(chosen.astype(F32))
    return ordered


def columns_of(pieces, start, columns):
    return jnp.concatenate([piece[:, start : start + columns] for piece in pieces], axis=1)


def total_over(value, axis, size):
    step = 1
    while step < size:
        value = value + lax.ppermute(value, axis, [(index, index ^ step) for index in range(size)])
        step *= 2
    return value


def flat(value):
    return value.reshape(-1, value.shape[-1])


def normalize(values):
    average = jnp.mean(values, axis=-1, keepdims=True)
    centred = values - average
    variance = jnp.mean(centred * centred, axis=-1, keepdims=True)
    rate = lax.rsqrt(variance + EPSILON)
    return centred * rate, rate


def norm_back(grad, normal, rate, gain):
    inner = grad * gain
    first = jnp.mean(inner, axis=-1, keepdims=True)
    second = jnp.mean(inner * normal, axis=-1, keepdims=True)
    back = (inner - first - normal * second) * rate
    return back, jnp.sum(grad * normal, axis=0), jnp.sum(grad, axis=0)


def gelu_parts(inner):
    share = 0.5 * (1.0 + lax.erf(inner * (0.5**0.5)))
    slope = share + inner * jnp.exp(-0.5 * inner * inner) * ((0.5 / jnp.pi) ** 0.5)
    return (inner * share).astype(BF16), slope.astype(BF16)


def head_major(weight):
    rows, width = weight.shape
    return weight.reshape(rows, BUCKETS, width // BUCKETS).transpose(0, 2, 1).reshape(rows, width)


def bucket_major(weight):
    rows, width = weight.shape
    return weight.reshape(rows, width // BUCKETS, BUCKETS).transpose(0, 2, 1).reshape(rows, width)


def body(
    ranks,
    shards,
    hidden,
    encoded,
    assign,
    bucket_table,
    w_query,
    w_key,
    w_value,
    w_rel,
    w_out,
    gain_one,
    shift_one,
    c_query,
    c_key,
    c_value,
    c_out,
    gain_two,
    shift_two,
    w_inner,
    w_outer,
    gain_three,
    shift_three,
    cotangent,
):
    seqs, rows, streams, width = hidden.shape
    seq = rows * ranks
    rank = lax.axis_index("ctx")
    slots = rows // BLK
    own_blocks = lax.dynamic_slice_in_dim(assign, rank * slots, slots)
    own = bucket_table[BLK - 1 : BLK]
    index = bucket_index(own_blocks, bucket_table, seq)
    hot = bucket_hots(bucket_table, seq, CHUNK)
    places = (assign[:, None] * BLK + jnp.arange(BLK, dtype=jnp.int32)[None, :]).reshape(-1)
    order = (places[None, :] == (seq - 1 - jnp.arange(seq, dtype=jnp.int32))[:, None]).astype(BF16)

    stacked = jnp.transpose(hidden, (2, 0, 1, 3))
    shape = stacked.shape
    parts = [w_key, w_value, w_query, head_major(w_rel)]
    full = gather(jnp.concatenate(parts, axis=1), ranks)
    main = gather_rows(hidden[:, :, 0, :], ranks)
    memory = gather_rows(encoded, ranks)
    main = jnp.einsum("mu,nud->nmd", order, main, preferred_element_type=F32).astype(BF16)
    norms = [gain_one, shift_one, gain_two, shift_two, gain_three, shift_three]
    norms = jnp.pad(jnp.stack(norms, axis=1), ((0, 0), (0, 122)))
    middle = jnp.concatenate([w_out, c_query, c_key, c_value, c_out, norms], axis=1)
    full, main, memory, stacked, middle, w_inner, w_outer = tie(
        full, main, memory, stacked, middle, w_inner, w_outer
    )
    middle = gather_pass(gather_half(middle, ranks), ranks)
    w_inner = gather_half(w_inner, ranks)
    w_outer = gather_half(w_outer, ranks)
    w_key, w_value, w_query = (full[:, start : start + width] for start in range(0, 3 * width, width))
    w_rel = full[:, 3 * width :]
    lines = flat(stacked)
    own_shape = (streams - 1,) + shape[1:]
    own_lines = flat(stacked[1:])
    main_lines = flat(main)
    main_shape = main.shape
    query = dot_nn(lines, w_query).astype(BF16).reshape(shape)
    rel = dot_nn(lines, w_rel).astype(BF16).reshape(shape[:-1] + (-1,))
    own_keys = dot_nn(own_lines, w_key).astype(BF16).reshape(own_shape)
    own_values = dot_nn(own_lines, w_value).astype(BF16).reshape(own_shape)
    keys = dot_nn(main_lines, w_key).astype(BF16).reshape(main_shape)
    values = dot_nn(main_lines, w_value).astype(BF16).reshape(main_shape)
    mixed, probs, own_probs = self_forward(
        own_blocks, own, query, rel, own_keys, own_values, keys, values, index
    )
    mixed, middle, w_inner, w_outer = tie(mixed, middle, w_inner, w_outer)
    w_inner = gather_pass(w_inner, ranks)
    w_outer = gather_pass(w_outer, ranks)
    full = gather_rest(middle, ranks)
    w_out, c_query, c_key, c_value, c_out = (
        full[:, start : start + width] for start in range(0, 5 * width, width)
    )
    norms = jnp.transpose(full[:, 5 * width :])[:6].astype(F32)
    gain_one, shift_one, gain_two, shift_two, gain_three, shift_three = (
        norms[index : index + 1] for index in range(6)
    )
    normal_one, rate_one = normalize(lines.astype(F32) + dot_nn(flat(mixed), w_out))
    h_one = normal_one * gain_one + shift_one
    h_one_low = h_one.astype(BF16)
    cross_query = dot_nn(h_one_low, c_query).astype(BF16).reshape(shape)
    memory_lines = flat(memory)
    cross_keys = dot_nn(memory_lines, c_key).astype(BF16).reshape(memory.shape)
    cross_values = dot_nn(memory_lines, c_value).astype(BF16).reshape(memory.shape)
    cross_mixed, cross_probs = cross_forward(cross_query, cross_keys, cross_values)
    cross_mixed, w_inner, w_outer = tie(cross_mixed, w_inner, w_outer)
    w_inner = gather_rest(w_inner, ranks)
    w_outer = gather_rest(w_outer, ranks)
    normal_two, rate_two = normalize(h_one + dot_nn(flat(cross_mixed), c_out))
    h_two = normal_two * gain_two + shift_two
    h_two_low = h_two.astype(BF16)
    active, slope = gelu_parts(dot_nn(h_two_low, w_inner))
    normal_three, rate_three = normalize(h_two + dot_nn(active, w_outer))
    output = (normal_three * gain_three + shift_three).astype(BF16)
    output = jnp.transpose(output.reshape(shape), (1, 2, 0, 3))

    grad = flat(jnp.transpose(cotangent, (2, 0, 1, 3))).astype(F32)
    grad_three, gain_three, shift_three = norm_back(grad, normal_three, rate_three, gain_three)
    grad_low = grad_three.astype(BF16)
    outer = Exchange(ranks, column_part(ranks, [(active, grad_low)]))
    outer.begin()
    grad_low = hold(grad_low, outer)
    grad_inner = (dot_nt(grad_low, w_outer) * slope.astype(F32)).astype(BF16)
    inner = Exchange(ranks, column_part(ranks, [(h_two_low, grad_inner)]))
    inner.begin()
    outer.turn()
    grad_inner = hold(grad_inner, inner, outer)
    outer.fetch()
    grad_h_two = grad_three + dot_nt(grad_inner, w_inner)
    grad_two, gain_two, shift_two = norm_back(grad_h_two, normal_two, rate_two, gain_two)
    c_out_low = grad_two.astype(BF16)
    inner.turn()
    grad_low = hold(c_out_low, inner)
    inner.fetch()
    grad_mixed = dot_nt(grad_low, c_out).astype(BF16).reshape(shape)
    cross_query_grad, key_grad, value_grad = cross_backward(
        cross_query, cross_keys, cross_values, cross_mixed, grad_mixed, cross_probs
    )
    cross_query_grad = hold(cross_query_grad, inner, outer)
    inner_total, outer_total = inner.end().astype(BF16), outer.end().astype(BF16)
    cross_query_grad, inner_total, outer_total = tie(cross_query_grad, inner_total, outer_total)
    depth = width // shards
    layers = outer_total.shape[0] // width
    outer_total = outer_total.reshape(shards, layers, depth, -1)
    parts = [outer_total[:, layer].reshape(width, -1) for layer in range(layers)]
    ffn_piece = scatter(jnp.concatenate([inner_total] + parts, axis=1))
    cross_query_grad = flat(cross_query_grad)
    key_grad, value_grad = flat(key_grad), flat(value_grad)
    grad_h_one = grad_two + dot_nt(cross_query_grad, c_query)
    grad_one, gain_one, shift_one = norm_back(grad_h_one, normal_one, rate_one, gain_one)
    grad_low = grad_one.astype(BF16)
    grad_mixed = dot_nt(grad_low, w_out).astype(BF16).reshape(shape)
    centre = Exchange(
        ranks,
        column_part(
            ranks,
            [(flat(mixed), grad_low)],
            [(h_one_low, cross_query_grad)],
            [(memory_lines, key_grad)],
            [(memory_lines, value_grad)],
            [(flat(cross_mixed), c_out_low)],
        ),
    )
    centre.begin()
    encoded_grad = (dot_nt(key_grad, c_key) + dot_nt(value_grad, c_value)).astype(BF16)
    centre.turn()
    memory_exchange = Exchange(ranks, block_part(ranks, encoded_grad.reshape(memory.shape)))
    memory_exchange.begin()
    norms = jnp.stack([gain_one, shift_one, gain_two, shift_two, gain_three, shift_three])
    grad_mixed, norms = hold(grad_mixed, centre, memory_exchange, norms)
    centre.fetch()
    memory_exchange.turn()
    memory_exchange.fetch()
    rank = lax.axis_index("ctx")
    steps = (3, 1, 2, 0)
    places = [rank ^ step if ranks == 4 else jnp.int32(index) for index, step in enumerate(steps)]
    back = {}

    def first_part(index, step):
        query_grad, rel_grad, own_key_grad, own_value_grad, key_grad, value_grad = back[step]
        own_grad = jnp.concatenate([own_key_grad, own_value_grad], axis=1)
        main_grad = jnp.concatenate([key_grad, value_grad], axis=1)
        return jnp.concatenate(
            [
                dot_tn(lines, query_grad),
                dot_tn(lines, rel_grad),
                dot_tn(own_lines, own_grad) + dot_tn(main_lines, main_grad),
            ],
            axis=1,
        )

    first = Exchange(ranks, first_part)
    for turn, step in enumerate(steps):
        results = self_backward(
            places[turn].reshape(1),
            own_blocks,
            own,
            query,
            own_keys,
            own_values,
            keys,
            values,
            hot,
            mixed,
            grad_mixed,
            probs,
            own_probs,
        )
        if turn < 3:
            grad_mixed, results = tie(grad_mixed, results)
        back[step] = [flat(value) for value in results]
        if turn == 1:
            if ranks == 4:
                first.begin()
            grad_mixed = hold(grad_mixed, centre, memory_exchange)
            centre_total = centre.end().astype(BF16)
            encoded_grad = memory_exchange.end()
            if ranks == 4:
                grad_mixed, centre_total = hold(grad_mixed, first, centre_total)
            centre_piece = scatter(centre_total)
        if turn == 2 and ranks == 4:
            first.turn()
            grad_mixed = hold(grad_mixed, first)
            first.fetch()
    joined = [jnp.concatenate(values, axis=1) for values in zip(*(back[step] for step in steps))]
    query_grad, rel_grad, own_key_grad, own_value_grad, key_grad, value_grad = joined
    if ranks == 4:
        back[0][0], key_grad = hold(back[0][0], first, key_grad)
        first_total = first.end().astype(BF16)
        key_grad, first_total = tie(key_grad, first_total)
    else:
        whole = column_part(
            ranks,
            [(lines, query_grad)],
            [(lines, rel_grad)],
            [(own_lines, own_key_grad), (main_lines, key_grad)],
            [(own_lines, own_value_grad), (main_lines, value_grad)],
        )
        first = Exchange(ranks, whole)
        first.begin()
        first_total = first.end().astype(BF16)
    first_piece = scatter(first_total)

    def reorder(weight):
        columns = weight.shape[1] // len(steps)
        return jnp.concatenate(
            [
                lax.dynamic_slice_in_dim(weight, index * columns, columns, axis=1)
                for index in places
            ],
            axis=1,
        )

    w_query, w_rel, w_key, w_value = (
        reorder(weight) for weight in (w_query, w_rel, w_key, w_value)
    )
    main_grad = (dot_nt(key_grad, w_key) + dot_nt(value_grad, w_value)).astype(BF16)
    main_grad = jnp.einsum(
        "mu,nmd->nud", order, main_grad.reshape(main_shape), preferred_element_type=F32
    ).astype(BF16)
    main_exchange = Exchange(ranks, block_part(ranks, main_grad))
    main_exchange.begin()
    main_exchange.turn()
    main_exchange.fetch()
    own_grad = dot_nt(own_key_grad, w_key) + dot_nt(own_value_grad, w_value)
    grad_lines = grad_one + dot_nt(query_grad, w_query)
    grad_lines = grad_lines + dot_nt(rel_grad, w_rel)
    grad_lines = grad_lines.reshape(shape) + jnp.concatenate(
        [main_exchange.end()[None], own_grad.reshape(own_shape)], axis=0
    )
    grad_hidden = jnp.transpose(grad_lines, (1, 2, 0, 3))
    norms = total_over(total_over(norms, "ctx", ranks), "fsdp", shards)
    count = norms.shape[1] // shards
    norms = lax.dynamic_slice_in_dim(norms, lax.axis_index("fsdp") * count, count, axis=1)
    gain_one, shift_one, gain_two, shift_two, gain_three, shift_three = (
        norms[index] for index in range(6)
    )
    pieces = collect(ranks, ffn_piece)
    columns = width // ranks
    cut = layers * columns
    w_inner_grad = columns_of(pieces, 0, cut)
    w_outer_grad = jnp.concatenate(
        [columns_of(pieces, cut + layer * columns, columns) for layer in range(layers)], axis=0
    )
    pieces = collect(ranks, centre_piece)
    w_out_grad, c_query_grad, c_key_grad, c_value_grad, c_out_grad = (
        columns_of(pieces, start * columns, columns) for start in range(5)
    )
    pieces = collect(ranks, first_piece)
    rel_columns = w_rel.shape[1] // ranks
    w_query_grad = columns_of(pieces, 0, columns)
    w_rel_grad = columns_of(pieces, columns, rel_columns)
    w_key_grad = columns_of(pieces, columns + rel_columns, columns)
    w_value_grad = columns_of(pieces, 2 * columns + rel_columns, columns)
    return (
        output,
        grad_hidden,
        encoded_grad,
        w_query_grad,
        w_key_grad,
        w_value_grad,
        bucket_major(w_rel_grad),
        w_out_grad,
        gain_one,
        shift_one,
        c_query_grad,
        c_key_grad,
        c_value_grad,
        c_out_grad,
        gain_two,
        shift_two,
        w_inner_grad,
        w_outer_grad,
        gain_three,
        shift_three,
    )


def solution(mesh):
    matrix, vector = P("fsdp", None), P("fsdp")
    rows = P("fsdp", "ctx", None, None)
    weights = (matrix,) * 5 + (vector,) * 2 + (matrix,) * 4 + (vector,) * 2 + (matrix,) * 2
    weights = weights + (vector,) * 2
    in_specs = (rows, P("fsdp", "ctx", None), P(), P()) + weights + (rows,)
    out_specs = (rows, rows, P("fsdp", "ctx", None)) + weights
    return jax.shard_map(
        functools.partial(body, mesh.shape["ctx"], mesh.shape["fsdp"]),
        mesh=mesh,
        in_specs=in_specs,
        out_specs=out_specs,
        check_vma=False,
    )
```

```python
import functools
import jax
import jax.numpy as jnp
from jax import lax
from jax.sharding import PartitionSpec as P
from jax.experimental import pallas as pl
from jax.experimental.pallas import tpu as pltpu

HEAD_DIM = 64
BUCKETS = 32
BLK = 32
CHUNK = 256
FILLER = -1e30
SCALE = HEAD_DIM ** (-0.5)
LIMIT = 60 * 1024 * 1024
F32 = jnp.float32
BF16 = jnp.bfloat16


def dot_nt(left, right):
    return lax.dot_general(left, right, (((1,), (1,)), ((), ())), preferred_element_type=F32)


def dot_tn(left, right):
    return lax.dot_general(left, right, (((0,), (0,)), ((), ())), preferred_element_type=F32)


def dot_nn(left, right):
    return jnp.dot(left, right, preferred_element_type=F32)


def low_lanes(rows):
    return lax.broadcasted_iota(jnp.int32, (rows, 128), 1) < HEAD_DIM


def pair_rows(value, low):
    zero = jnp.zeros_like(value)
    return jnp.concatenate([jnp.where(low, value, zero), jnp.where(low, zero, value)], axis=0)


def self_parts(slot, pair, query_ref, own_key_ref, own_value_ref):
    rows = pl.ds(pl.multiple_of(slot * BLK, BLK), BLK)
    lanes = slice(128 * pair, 128 * (pair + 1))
    total = query_ref.shape[0] * BLK
    low = low_lanes(total)
    query = query_ref[:, 0, rows, lanes].reshape(total, 128)
    pairs = pair_rows(query, low) * jnp.asarray(SCALE, BF16)
    zero = jnp.zeros((BLK, 128), F32)
    own_key = own_key_ref[:, 0, rows, lanes].reshape(total - BLK, 128).astype(F32)
    own_key = jnp.concatenate([zero, own_key], axis=0)
    own_value = own_value_ref[:, 0, rows, lanes].reshape(total - BLK, 128).astype(F32)
    own_value = jnp.concatenate([zero, own_value], axis=0)
    return rows, lanes, low, pairs, own_key, own_value


def slot_pairs(blocks, seq, work):
    def step(place, carry):
        first, second = blocks[2 * place], blocks[2 * place + 1]
        turned = (first > second).astype(jnp.int32)
        near, far = 2 * place + turned, 2 * place + 1 - turned
        near_block, far_block = jnp.minimum(first, second), jnp.maximum(first, second)
        whole = seq // CHUNK
        count = (near_block * BLK) // CHUNK + 1
        for parts in range(1, whole // 2 + 1):

            @pl.when(count == parts)
            def _():
                work(
                    [
                        (slot, block, pair, chunks * CHUNK)
                        for slot, block, chunks in (
                            (near, near_block, parts),
                            (far, far_block, whole + 1 - parts),
                        )
                        for pair in range(2)
                    ]
                )

        return carry

    lax.fori_loop(0, blocks.shape[0] // 2, step, 0)


def self_forward_kernel(
    blocks,
    own_ref,
    query_ref,
    rel_ref,
    own_key_ref,
    own_value_ref,
    key_ref,
    value_ref,
    index_ref,
    out_ref,
    prob_ref,
    own_prob_ref,
):
    seq = key_ref.shape[1]
    streams = query_ref.shape[0]
    total = streams * BLK

    def scored(slot, block, pair, width):
        rows, lanes, low, pairs, own_key, own_value = self_parts(
            slot, pair, query_ref, own_key_ref, own_value_ref
        )
        span = slice(seq - width, seq)
        rel = rel_ref[:, 0, rows, :].reshape(total, 128).astype(F32)
        first = pltpu.roll(rel, 64, 1) if pair else rel
        table = jnp.concatenate([first, pltpu.roll(rel, 32 if pair else 96, 1)], axis=0)
        lane = lax.broadcasted_iota(jnp.int32, (2 * total, 128), 1)
        own = jnp.where(lane == own_ref[0], table, 0.0)
        own = own + pairs.astype(F32) * jnp.concatenate([own_key, own_key], axis=0)
        own = jnp.sum(own, axis=1, keepdims=True)
        row = lax.broadcasted_iota(jnp.int32, (2 * total, 1), 0)
        main = jnp.logical_or(row < BLK, jnp.logical_and(row >= total, row < total + BLK))
        own = jnp.where(main, FILLER, own)
        index = index_ref[rows, span]
        bias = [
            jnp.take_along_axis(
                table,
                jnp.concatenate([index[:, start : start + 128]] * (2 * streams), axis=0),
                axis=1,
            )
            for start in range(0, width, 128)
        ]
        scores = dot_nt(pairs, key_ref[0, span, lanes]) + jnp.concatenate(bias, axis=1)
        column = lax.broadcasted_iota(jnp.int32, (2 * total, CHUNK), 1)
        seen = column >= width - BLK * (block + 1)
        first = jnp.where(seen, scores[:, :CHUNK], FILLER)
        scores = first if width == CHUNK else jnp.concatenate([first, scores[:, CHUNK:]], axis=1)
        top = jnp.maximum(jnp.max(scores, axis=1, keepdims=True), own)
        return scores, own, top, own_value

    def work(items):
        stage = [scored(*item) for item in items]
        stage = [
            (jnp.exp(scores - top), jnp.exp(own - top), own_value)
            for scores, own, top, own_value in stage
        ]
        stage = [
            (weights, own, 1.0 / (jnp.sum(weights, axis=1, keepdims=True) + own), own_value)
            for weights, own, own_value in stage
        ]
        low = low_lanes(total)
        for (slot, block, pair, width), (weights, own, inverse, own_value) in zip(items, stage):
            rows = pl.ds(pl.multiple_of(slot * BLK, BLK), BLK)
            lanes = slice(128 * pair, 128 * (pair + 1))
            span = slice(seq - width, seq)
            probs = (weights * inverse).astype(BF16)
            prob_ref[0, pair, slot, :, span] = probs
            own_prob = own * inverse
            own_prob_ref[0, pair, slot] = jnp.broadcast_to(own_prob, (2 * total, 128)).astype(BF16)
            mixed = dot_nn(probs, value_ref[0, span, lanes])
            result = jnp.where(
                low,
                mixed[:total] + own_prob[:total] * own_value,
                mixed[total:] + own_prob[total:] * own_value,
            )
            out_ref[:, 0, rows, lanes] = result.astype(BF16).reshape(streams, BLK, 128)

    slot_pairs(blocks, seq, work)


def self_backward_kernel(
    group,
    blocks,
    own_ref,
    query_ref,
    own_key_ref,
    own_value_ref,
    key_ref,
    value_ref,
    hot_ref,
    out_ref,
    grad_ref,
    prob_ref,
    own_prob_ref,
    grad_query_ref,
    grad_rel_ref,
    grad_own_key_ref,
    grad_own_value_ref,
    grad_key_ref,
    grad_value_ref,
    key_total,
    value_total,
):
    seq = key_ref.shape[1]
    streams = query_ref.shape[0]
    total = streams * BLK
    key_total[...] = jnp.zeros_like(key_total)
    value_total[...] = jnp.zeros_like(value_total)

    def scored(slot, block, pair, width):
        rows, lanes, low, pairs, own_key, own_value = self_parts(
            slot, pair, query_ref, own_key_ref, own_value_ref
        )
        span = slice(seq - width, seq)
        grads = pair_rows(grad_ref[:, 0, rows, lanes].reshape(total, 128), low)
        wide = grads.astype(F32)
        mixed = out_ref[:, 0, rows, lanes].reshape(total, 128).astype(F32)
        delta = jnp.sum(wide * jnp.concatenate([mixed, mixed], axis=0), axis=1, keepdims=True)
        grad_own = jnp.sum(
            wide * jnp.concatenate([own_value, own_value], axis=0), axis=1, keepdims=True
        )
        own_prob = own_prob_ref[0, pair, slot].astype(F32)
        grad_own = own_prob * (grad_own - delta)
        part = grad_own * pairs.astype(F32)
        part = (part[:total] + part[total:])[BLK:]
        grad_own_key_ref[:, 0, rows, lanes] = part.astype(BF16).reshape(streams - 1, BLK, 128)
        part = own_prob * wide
        part = (part[:total] + part[total:])[BLK:]
        grad_own_value_ref[:, 0, rows, lanes] = part.astype(BF16).reshape(streams - 1, BLK, 128)
        probs = prob_ref[0, pair, slot, :, span]
        grad_probs = dot_nt(grads, value_ref[0, span, lanes])
        grad_scores = probs.astype(F32) * (grad_probs - delta)
        return pairs, grads, own_key, grad_own, probs, grad_scores

    def skew(block, width, grad_scores, grad_own):
        pad = jnp.zeros((BLK, 128), F32)
        skewed = []
        for start in range(0, 2 * total, BLK):
            piece = jnp.concatenate([grad_scores[start : start + BLK], pad], axis=1)
            skewed.append(pltpu.roll(piece, 0, 1, stride=1, stride_axis=0).astype(BF16))
        begin = pl.multiple_of(BLK * (block + 1) - width + CHUNK, BLK)
        sums = dot_nn(jnp.concatenate(skewed, axis=0), hot_ref[pl.ds(begin, width + 128), :])
        lane = lax.broadcasted_iota(jnp.int32, (2 * total, 128), 1)
        return sums + jnp.where(lane == own_ref[0], grad_own, 0.0)

    def work(items):
        stage = [scored(*item) for item in items]
        low = low_lanes(total)
        sums = []
        for (slot, block, pair, width), values in zip(items, stage):
            pairs, grads, own_key, grad_own, probs, grad_scores = values
            rows = pl.ds(pl.multiple_of(slot * BLK, BLK), BLK)
            lanes = slice(128 * pair, 128 * (pair + 1))
            span = slice(seq - width, seq)
            low_scores = grad_scores.astype(BF16)
            value_total[span, lanes] += dot_tn(probs, grads)
            key_total[span, lanes] += dot_tn(low_scores, pairs)
            moved = dot_nn(low_scores, key_ref[0, span, lanes])
            moved = jnp.where(
                low,
                moved[:total] + grad_own[:total] * own_key,
                moved[total:] + grad_own[total:] * own_key,
            )
            grad_query_ref[:, 0, rows, lanes] = (
                (moved * SCALE).astype(BF16).reshape(streams, BLK, 128)
            )
            sums.append(skew(block, width, grad_scores, grad_own))
        for place in range(0, len(items), 2):
            slot = items[place][0]
            rows = pl.ds(pl.multiple_of(slot * BLK, BLK), BLK)
            result = sums[place][:total] + pltpu.roll(sums[place][total:], BUCKETS, 1)
            result = result + pltpu.roll(sums[place + 1][:total], 2 * BUCKETS, 1)
            result = result + pltpu.roll(sums[place + 1][total:], 3 * BUCKETS, 1)
            grad_rel_ref[:, 0, rows, :] = result.astype(BF16).reshape(streams, BLK, 128)

    slot_pairs(blocks, seq, work)
    grad_key_ref[0] = key_total[...].astype(BF16)
    grad_value_ref[0] = value_total[...].astype(BF16)


def group_spec(streams, rows, lanes):
    return pl.BlockSpec((streams, 1, rows, lanes), lambda n, g: (0, n, 0, g))


def full_spec(rows, lanes):
    return pl.BlockSpec((1, rows, lanes), lambda n, g: (n, 0, g))


def smem_spec():
    return pl.BlockSpec(memory_space=pltpu.SMEM)


def estimate(flops, moved):
    return pl.CostEstimate(flops=int(flops), bytes_accessed=int(moved), transcendentals=0)


def prob_spec(slots, total, width):
    return pl.BlockSpec((1, 2, slots, total, width), lambda n, g: (n, g, 0, 0, 0))


def whole_spec(value):
    return pl.BlockSpec(value.shape, lambda n, g: (0,) * value.ndim)


def self_forward(blocks, own, query, rel, own_key, own_value, keys, values, index):
    streams, seqs, rows, width = query.shape
    seq = keys.shape[1]
    slots = rows // BLK
    total = 2 * streams * BLK
    return pl.pallas_call(
        self_forward_kernel,
        grid=(seqs, width // 256),
        in_specs=[
            smem_spec(),
            smem_spec(),
            group_spec(streams, rows, 256),
            group_spec(streams, rows, 128),
            group_spec(streams - 1, rows, 256),
            group_spec(streams - 1, rows, 256),
            full_spec(seq, 256),
            full_spec(seq, 256),
            whole_spec(index),
        ],
        out_specs=[
            group_spec(streams, rows, 256),
            prob_spec(slots, total, seq),
            prob_spec(slots, total, 128),
        ],
        out_shape=[
            jax.ShapeDtypeStruct(query.shape, BF16),
            jax.ShapeDtypeStruct((seqs, width // 128, slots, total, seq), BF16),
            jax.ShapeDtypeStruct((seqs, width // 128, slots, total, 128), BF16),
        ],
        compiler_params=pltpu.CompilerParams(vmem_limit_bytes=LIMIT),
        cost_estimate=estimate(88e9, 80e6),
        name="self_forward",
    )(blocks, own, query, rel, own_key, own_value, keys, values, index)


def self_backward(
    group, blocks, own, query, own_key, own_value, keys, values, hot, mixed, grad, probs, own_probs
):
    streams, seqs, rows, width = query.shape
    seq = keys.shape[1]
    slots = rows // BLK
    total = 2 * streams * BLK

    def lines(count):
        return pl.BlockSpec((count, 1, rows, 256), lambda n, g, b, o: (0, n, 0, g[0]))

    def result(count, lanes):
        return pl.BlockSpec((count, 1, rows, lanes), lambda n, g, b, o: (0, n, 0, 0))

    def shape(count, lanes):
        return jax.ShapeDtypeStruct((count, seqs, rows, lanes), BF16)

    def stored(lanes):
        return pl.BlockSpec((1, 2, slots, total, lanes), lambda n, g, b, o: (n, g[0], 0, 0, 0))

    memory = pl.BlockSpec((1, seq, 256), lambda n, g, b, o: (n, 0, g[0]))
    memory_result = pl.BlockSpec((1, seq, 256), lambda n, g, b, o: (n, 0, 0))
    memory_shape = jax.ShapeDtypeStruct((seqs, seq, 256), BF16)
    return pl.pallas_call(
        self_backward_kernel,
        grid_spec=pltpu.PrefetchScalarGridSpec(
            num_scalar_prefetch=3,
            grid=(seqs,),
            in_specs=[
                lines(streams),
                lines(streams - 1),
                lines(streams - 1),
                memory,
                memory,
                pl.BlockSpec(hot.shape, lambda n, g, b, o: (0, 0)),
                lines(streams),
                lines(streams),
                stored(seq),
                stored(128),
            ],
            out_specs=[
                result(streams, 256),
                result(streams, 128),
                result(streams - 1, 256),
                result(streams - 1, 256),
                memory_result,
                memory_result,
            ],
            scratch_shapes=[pltpu.VMEM((seq, 256), F32), pltpu.VMEM((seq, 256), F32)],
        ),
        out_shape=[
            shape(streams, 256),
            shape(streams, 128),
            shape(streams - 1, 256),
            shape(streams - 1, 256),
            memory_shape,
            memory_shape,
        ],
        compiler_params=pltpu.CompilerParams(vmem_limit_bytes=LIMIT),
        cost_estimate=estimate(27e9, 25e6),
        name="self_backward",
    )(group, blocks, own, query, own_key, own_value, keys, values, hot, mixed, grad, probs, own_probs)


def cross_forward_kernel(query_ref, key_ref, value_ref, out_ref, prob_ref):
    rows = query_ref.shape[2]
    low = low_lanes(rows)
    for pair in range(2):
        lanes = slice(128 * pair, 128 * pair + 128)
        pairs = pair_rows(query_ref[0, 0, :, lanes], low) * jnp.asarray(SCALE, BF16)
        scores = dot_nt(pairs, key_ref[0, :, lanes])
        top = jnp.max(scores, axis=1, keepdims=True)
        weights = jnp.exp(scores - top)
        inverse = 1.0 / jnp.sum(weights, axis=1, keepdims=True)
        probs = (weights * inverse).astype(BF16)
        prob_ref[0, 0, pair] = probs
        mixed = dot_nn(probs, value_ref[0, :, lanes])
        out_ref[0, 0, :, lanes] = jnp.where(low, mixed[:rows], mixed[rows:]).astype(BF16)


def cross_backward_kernel(
    query_ref,
    key_ref,
    value_ref,
    out_ref,
    grad_ref,
    prob_ref,
    grad_query_ref,
    grad_key_ref,
    grad_value_ref,
    key_total,
    value_total,
):
    rows = query_ref.shape[2]
    low = low_lanes(rows)
    stream = pl.program_id(2)

    @pl.when(stream == 0)
    def _():
        key_total[...] = jnp.zeros_like(key_total)
        value_total[...] = jnp.zeros_like(value_total)

    for pair in range(2):
        lanes = slice(128 * pair, 128 * pair + 128)
        pairs = pair_rows(query_ref[0, 0, :, lanes], low) * jnp.asarray(SCALE, BF16)
        keys = key_ref[0, :, lanes]
        grads = pair_rows(grad_ref[0, 0, :, lanes], low)
        mixed = out_ref[0, 0, :, lanes].astype(F32)
        delta = jnp.sum(
            grads.astype(F32) * jnp.concatenate([mixed, mixed], axis=0), axis=1, keepdims=True
        )
        probs = prob_ref[0, 0, pair]
        grad_probs = dot_nt(grads, value_ref[0, :, lanes])
        grad_scores = (probs.astype(F32) * (grad_probs - delta)).astype(BF16)
        value_total[:, lanes] += dot_tn(probs, grads)
        key_total[:, lanes] += dot_tn(grad_scores, pairs)
        moved = dot_nn(grad_scores, keys) * SCALE
        grad_query_ref[0, 0, :, lanes] = jnp.where(low, moved[:rows], moved[rows:]).astype(BF16)

    @pl.when(stream == pl.num_programs(2) - 1)
    def _():
        grad_key_ref[0] = key_total[...].astype(BF16)
        grad_value_ref[0] = value_total[...].astype(BF16)


def stream_spec(rows):
    return pl.BlockSpec((1, 1, rows, 256), lambda n, g, s: (s, n, 0, g))


def memory_spec(rows):
    return pl.BlockSpec((1, rows, 256), lambda n, g, s: (n, 0, g))


def cross_prob_spec(rows, memory):
    return pl.BlockSpec((1, 1, 2, 2 * rows, memory), lambda n, g, s: (s, n, g, 0, 0))


def cross_forward(query, keys, values):
    streams, seqs, rows, width = query.shape
    memory = keys.shape[1]
    return pl.pallas_call(
        cross_forward_kernel,
        grid=(seqs, width // 256, streams),
        in_specs=[stream_spec(rows), memory_spec(memory), memory_spec(memory)],
        out_specs=[stream_spec(rows), cross_prob_spec(rows, memory)],
        out_shape=[
            jax.ShapeDtypeStruct(query.shape, BF16),
            jax.ShapeDtypeStruct((streams, seqs, width // 128, 2 * rows, memory), BF16),
        ],
        compiler_params=pltpu.CompilerParams(vmem_limit_bytes=LIMIT),
        cost_estimate=estimate(38e9, 40e6),
        name="cross_forward",
    )(query, keys, values)


def cross_backward(query, keys, values, mixed, grad, probs):
    streams, seqs, rows, width = query.shape
    memory = keys.shape[1]
    return pl.pallas_call(
        cross_backward_kernel,
        grid=(seqs, width // 256, streams),
        in_specs=[
            stream_spec(rows),
            memory_spec(memory),
            memory_spec(memory),
            stream_spec(rows),
            stream_spec(rows),
            cross_prob_spec(rows, memory),
        ],
        out_specs=[stream_spec(rows), memory_spec(memory), memory_spec(memory)],
        out_shape=[
            jax.ShapeDtypeStruct(query.shape, BF16),
            jax.ShapeDtypeStruct(keys.shape, BF16),
            jax.ShapeDtypeStruct(keys.shape, BF16),
        ],
        scratch_shapes=[pltpu.VMEM((memory, 256), F32), pltpu.VMEM((memory, 256), F32)],
        compiler_params=pltpu.CompilerParams(vmem_limit_bytes=LIMIT),
        cost_estimate=estimate(47e9, 50e6),
        name="cross_backward",
    )(query, keys, values, mixed, grad, probs)


def bucket_index(own_blocks, bucket_table, seq):
    span = bucket_table.shape[0]
    front = seq - BLK
    length = 2 * seq + BLK
    line = jnp.zeros((length,), jnp.int32).at[front : front + span].set(bucket_table)
    flat = jnp.tile(line, BLK + 1)[: BLK * (length + 1)]
    skew = flat.reshape(BLK, length + 1)
    parts = [
        lax.dynamic_slice_in_dim(skew, own_blocks[slot] * BLK, seq, axis=1)
        for slot in range(own_blocks.shape[0])
    ]
    return jnp.concatenate(parts, axis=0)


def bucket_hots(bucket_table, seq, front):
    span = bucket_table.shape[0]
    depth = CHUNK + seq + 128
    line = jnp.full((front + span + depth,), -1, jnp.int32)
    line = line.at[front : front + span].set(bucket_table)[:depth]
    lane = jnp.arange(128, dtype=jnp.int32)
    return (line[:, None] == lane[None, :]).astype(BF16)


EPSILON = 1e-05
FULL = ("fsdp", "ctx")


PARTNER = [(0, 1), (1, 0), (2, 3), (3, 2)]
ACROSS = [(0, 2), (2, 0), (1, 3), (3, 1)]


def gather(shard, ranks):
    rows = shard.shape[0] // ranks
    piece = lax.dynamic_slice_in_dim(shard, lax.axis_index("ctx") * rows, rows)
    return lax.all_gather(piece, FULL, axis=0, tiled=True)


def swap(value):
    return lax.ppermute(value, "ctx", PARTNER)


def pass_across(value):
    return lax.ppermute(value, "ctx", ACROSS)


def tie(*values):
    return lax.optimization_barrier(values)


def spread(piece):
    across = pass_across(piece)
    return piece, swap(piece), across, swap(across)


def place_kernel(rank, first, second, third, fourth, out_ref):
    for step, ref in enumerate((first, second, third, fourth)):

        @pl.when((rank[0] ^ step) == pl.program_id(0))
        def _():
            out_ref[:, 0] = ref[...]


def place(pieces):
    outer, rows, columns = pieces[0].shape
    return pl.pallas_call(
        place_kernel,
        grid=(4,),
        in_specs=[smem_spec()] + [whole_block(piece) for piece in pieces],
        out_specs=pl.BlockSpec((outer, 1, rows, columns), lambda step: (0, step, 0, 0)),
        out_shape=jax.ShapeDtypeStruct((outer, 4, rows, columns), pieces[0].dtype),
        compiler_params=pltpu.CompilerParams(vmem_limit_bytes=LIMIT),
        cost_estimate=estimate(0, 8 * pieces[0].size * 2),
        name="place",
    )(lax.axis_index("ctx").reshape(1), *pieces)


def whole_block(value):
    return pl.BlockSpec(
        value.shape, lambda step: (0,) * value.ndim, pipeline_mode=pl.Buffered(1)
    )


def gather_half(shard, ranks):
    if ranks != 4:
        return gather(shard, ranks)
    rows = shard.shape[0] // ranks
    piece = lax.dynamic_slice_in_dim(shard, lax.axis_index("ctx") * rows, rows)
    return lax.all_gather(piece, "fsdp", axis=0, tiled=False)


def gather_pass(piece, ranks):
    if ranks != 4:
        return (piece,)
    return piece, swap(piece), pass_across(piece)


def gather_rest(pieces, ranks):
    if ranks != 4:
        return pieces[0]
    piece, partner, across = pieces
    return place((piece, partner, across, swap(across))).reshape(-1, piece.shape[2])


def gather_rows(value, ranks):
    if ranks != 4:
        return lax.all_gather(value, "ctx", axis=1, tiled=True)
    return place(spread(value)).reshape(value.shape[0], -1, value.shape[2])


def column_part(count, *groups):
    def part(index, step):
        parts = []
        for group in groups:
            total = 0.0
            for left, right in group:
                columns = right.shape[1] // count
                right = lax.dynamic_slice_in_dim(right, index * columns, columns, axis=1)
                total = total + dot_tn(left, right)
            parts.append(total)
        return parts[0] if len(parts) == 1 else jnp.concatenate(parts, axis=1)

    return part


def block_part(count, value):
    rows = value.shape[1] // count

    def part(index, step):
        return lax.dynamic_slice_in_dim(value, index * rows, rows, axis=1).astype(F32)

    return part


class Exchange:
    def __init__(self, ranks, part):
        self.ranks = ranks
        self.part = part
        self.rank = lax.axis_index("ctx")

    def begin(self, both=True):
        if self.ranks != 4:
            every = [self.part(index, index).astype(BF16) for index in range(self.ranks)]
            self.values = (jnp.stack(every),)
            return
        self.values = (self.part(self.rank ^ 3, 3).astype(BF16),)
        if both:
            self.late()

    def late(self):
        self.values = self.values + (self.part(self.rank ^ 1, 1).astype(BF16),)

    def turn(self):
        if self.ranks != 4:
            return
        corner, partner = swap(self.values[0]), self.values[1:]
        side = (self.part(self.rank ^ 2, 2) + corner.astype(F32)).astype(BF16)
        self.values = (side,) + tuple(swap(value) for value in partner)

    def fetch(self):
        if self.ranks == 4:
            self.values = (pass_across(self.values[0]),) + self.values[1:]

    def end(self):
        if self.ranks != 4:
            mine = lax.psum_scatter(self.values[0], "ctx", scatter_dimension=0, tiled=True)
            return mine[0].astype(F32)
        side, partner = self.values
        return self.part(self.rank, 0) + partner.astype(F32) + side.astype(F32)


def hold(value, *items):
    packed = [item.values if isinstance(item, Exchange) else item for item in items]
    value, packed = tie(value, packed)
    for item, new in zip(items, packed):
        if isinstance(item, Exchange):
            item.values = new
    others = [new for item, new in zip(items, packed) if not isinstance(item, Exchange)]
    return (value, *others) if others else value


def scatter(total):
    return lax.psum_scatter(total.astype(BF16), "fsdp", scatter_dimension=0, tiled=True)


def collect(ranks, piece):
    if ranks != 4:
        whole = lax.all_gather(piece, "ctx", axis=0, tiled=False)
        return [whole[index].astype(F32) for index in range(ranks)]
    rank = lax.axis_index("ctx")
    pieces = spread(piece)
    ordered = []
    for index in range(4):
        chosen = pieces[3]
        for step in range(3):
            chosen = jnp.where((rank ^ step) == index, pieces[step], chosen)
        ordered.append(chosen.astype(F32))
    return ordered


def columns_of(pieces, start, columns):
    return jnp.concatenate([piece[:, start : start + columns] for piece in pieces], axis=1)


def total_over(value, axis, size):
    step = 1
    while step < size:
        value = value + lax.ppermute(value, axis, [(index, index ^ step) for index in range(size)])
        step *= 2
    return value


def flat(value):
    return value.reshape(-1, value.shape[-1])


def normalize(values):
    average = jnp.mean(values, axis=-1, keepdims=True)
    centred = values - average
    variance = jnp.mean(centred * centred, axis=-1, keepdims=True)
    rate = lax.rsqrt(variance + EPSILON)
    return centred * rate, rate


def norm_back(grad, normal, rate, gain):
    inner = grad * gain
    first = jnp.mean(inner, axis=-1, keepdims=True)
    second = jnp.mean(inner * normal, axis=-1, keepdims=True)
    back = (inner - first - normal * second) * rate
    return back, jnp.sum(grad * normal, axis=0), jnp.sum(grad, axis=0)


def gelu_parts(inner):
    share = 0.5 * (1.0 + lax.erf(inner * (0.5**0.5)))
    slope = share + inner * jnp.exp(-0.5 * inner * inner) * ((0.5 / jnp.pi) ** 0.5)
    return (inner * share).astype(BF16), slope.astype(BF16)


def head_major(weight):
    rows, width = weight.shape
    return weight.reshape(rows, BUCKETS, width // BUCKETS).transpose(0, 2, 1).reshape(rows, width)


def bucket_major(weight):
    rows, width = weight.shape
    return weight.reshape(rows, width // BUCKETS, BUCKETS).transpose(0, 2, 1).reshape(rows, width)


def body(
    ranks,
    shards,
    hidden,
    encoded,
    assign,
    bucket_table,
    w_query,
    w_key,
    w_value,
    w_rel,
    w_out,
    gain_one,
    shift_one,
    c_query,
    c_key,
    c_value,
    c_out,
    gain_two,
    shift_two,
    w_inner,
    w_outer,
    gain_three,
    shift_three,
    cotangent,
):
    seqs, rows, streams, width = hidden.shape
    seq = rows * ranks
    rank = lax.axis_index("ctx")
    slots = rows // BLK
    own_blocks = lax.dynamic_slice_in_dim(assign, rank * slots, slots)
    own = bucket_table[BLK - 1 : BLK]
    index = bucket_index(own_blocks, bucket_table, seq)
    hot = bucket_hots(bucket_table, seq, CHUNK)
    places = (assign[:, None] * BLK + jnp.arange(BLK, dtype=jnp.int32)[None, :]).reshape(-1)
    order = (places[None, :] == (seq - 1 - jnp.arange(seq, dtype=jnp.int32))[:, None]).astype(BF16)

    stacked = jnp.transpose(hidden, (2, 0, 1, 3))
    shape = stacked.shape
    parts = [w_key, w_value, w_query, head_major(w_rel)]
    full = gather(jnp.concatenate(parts, axis=1), ranks)
    main = gather_rows(hidden[:, :, 0, :], ranks)
    memory = gather_rows(encoded, ranks)
    main = jnp.einsum("mu,nud->nmd", order, main, preferred_element_type=F32).astype(BF16)
    norms = [gain_one, shift_one, gain_two, shift_two, gain_three, shift_three]
    norms = jnp.pad(jnp.stack(norms, axis=1), ((0, 0), (0, 122)))
    middle = jnp.concatenate([w_out, c_query, c_key, c_value, c_out, norms], axis=1)
    full, main, memory, stacked, middle, w_inner, w_outer = tie(
        full, main, memory, stacked, middle, w_inner, w_outer
    )
    middle = gather_pass(gather_half(middle, ranks), ranks)
    w_inner = gather_half(w_inner, ranks)
    w_outer = gather_half(w_outer, ranks)
    w_key, w_value, w_query = (full[:, start : start + width] for start in range(0, 3 * width, width))
    w_rel = full[:, 3 * width :]
    lines = flat(stacked)
    own_shape = (streams - 1,) + shape[1:]
    own_lines = flat(stacked[1:])
    main_lines = flat(main)
    main_shape = main.shape
    query = dot_nn(lines, w_query).astype(BF16).reshape(shape)
    rel = dot_nn(lines, w_rel).astype(BF16).reshape(shape[:-1] + (-1,))
    own_keys = dot_nn(own_lines, w_key).astype(BF16).reshape(own_shape)
    own_values = dot_nn(own_lines, w_value).astype(BF16).reshape(own_shape)
    keys = dot_nn(main_lines, w_key).astype(BF16).reshape(main_shape)
    values = dot_nn(main_lines, w_value).astype(BF16).reshape(main_shape)
    mixed, probs, own_probs = self_forward(
        own_blocks, own, query, rel, own_keys, own_values, keys, values, index
    )
    mixed, middle, w_inner = tie(mixed, middle, w_inner)
    w_inner = gather_pass(w_inner, ranks)
    full = gather_rest(middle, ranks)
    w_out, c_query, c_key, c_value, c_out = (
        full[:, start : start + width] for start in range(0, 5 * width, width)
    )
    norms = jnp.transpose(full[:, 5 * width :])[:6].astype(F32)
    gain_one, shift_one, gain_two, shift_two, gain_three, shift_three = (
        norms[index : index + 1] for index in range(6)
    )
    normal_one, rate_one = normalize(lines.astype(F32) + dot_nn(flat(mixed), w_out))
    h_one = normal_one * gain_one + shift_one
    h_one_low = h_one.astype(BF16)
    cross_query = dot_nn(h_one_low, c_query).astype(BF16).reshape(shape)
    cross_query, w_outer = tie(cross_query, w_outer)
    w_outer = gather_pass(w_outer, ranks)
    memory_lines = flat(memory)
    cross_keys = dot_nn(memory_lines, c_key).astype(BF16).reshape(memory.shape)
    cross_values = dot_nn(memory_lines, c_value).astype(BF16).reshape(memory.shape)
    cross_mixed, cross_probs = cross_forward(cross_query, cross_keys, cross_values)
    cross_mixed, w_inner = tie(cross_mixed, w_inner)
    w_inner = gather_rest(w_inner, ranks)
    normal_two, rate_two = normalize(h_one + dot_nn(flat(cross_mixed), c_out))
    h_two = normal_two * gain_two + shift_two
    h_two_low = h_two.astype(BF16)
    active, slope = gelu_parts(dot_nn(h_two_low, w_inner))
    active, w_outer = tie(active, w_outer)
    w_outer = gather_rest(w_outer, ranks)
    normal_three, rate_three = normalize(h_two + dot_nn(active, w_outer))
    output = (normal_three * gain_three + shift_three).astype(BF16)
    output = jnp.transpose(output.reshape(shape), (1, 2, 0, 3))

    grad = flat(jnp.transpose(cotangent, (2, 0, 1, 3))).astype(F32)
    grad_three, gain_three, shift_three = norm_back(grad, normal_three, rate_three, gain_three)
    grad_low = grad_three.astype(BF16)
    outer = Exchange(ranks, column_part(ranks, [(active, grad_low)]))
    outer.begin()
    grad_low = hold(grad_low, outer)
    grad_inner = (dot_nt(grad_low, w_outer) * slope.astype(F32)).astype(BF16)
    inner = Exchange(ranks, column_part(ranks, [(h_two_low, grad_inner)]))
    inner.begin()
    outer.turn()
    grad_inner = hold(grad_inner, inner, outer)
    outer.fetch()
    grad_h_two = grad_three + dot_nt(grad_inner, w_inner)
    grad_two, gain_two, shift_two = norm_back(grad_h_two, normal_two, rate_two, gain_two)
    c_out_low = grad_two.astype(BF16)
    inner.turn()
    grad_low = hold(c_out_low, inner)
    inner.fetch()
    grad_mixed = dot_nt(grad_low, c_out).astype(BF16).reshape(shape)
    cross_query_grad, key_grad, value_grad = cross_backward(
        cross_query, cross_keys, cross_values, cross_mixed, grad_mixed, cross_probs
    )
    cross_query_grad = hold(cross_query_grad, inner, outer)
    inner_total, outer_total = inner.end().astype(BF16), outer.end().astype(BF16)
    cross_query_grad, inner_total, outer_total = tie(cross_query_grad, inner_total, outer_total)
    depth = width // shards
    layers = outer_total.shape[0] // width
    outer_total = outer_total.reshape(shards, layers, depth, -1)
    parts = [outer_total[:, layer].reshape(width, -1) for layer in range(layers)]
    ffn_piece = scatter(jnp.concatenate([inner_total] + parts, axis=1))
    cross_query_grad = flat(cross_query_grad)
    key_grad, value_grad = flat(key_grad), flat(value_grad)
    grad_h_one = grad_two + dot_nt(cross_query_grad, c_query)
    grad_one, gain_one, shift_one = norm_back(grad_h_one, normal_one, rate_one, gain_one)
    grad_low = grad_one.astype(BF16)
    grad_mixed = dot_nt(grad_low, w_out).astype(BF16).reshape(shape)
    centre = Exchange(
        ranks,
        column_part(
            ranks,
            [(flat(mixed), grad_low)],
            [(h_one_low, cross_query_grad)],
            [(memory_lines, key_grad)],
            [(memory_lines, value_grad)],
            [(flat(cross_mixed), c_out_low)],
        ),
    )
    centre.begin()
    encoded_grad = (dot_nt(key_grad, c_key) + dot_nt(value_grad, c_value)).astype(BF16)
    centre.turn()
    memory_exchange = Exchange(ranks, block_part(ranks, encoded_grad.reshape(memory.shape)))
    memory_exchange.begin()
    norms = jnp.stack([gain_one, shift_one, gain_two, shift_two, gain_three, shift_three])
    grad_mixed, norms = hold(grad_mixed, centre, memory_exchange, norms)
    centre.fetch()
    memory_exchange.turn()
    memory_exchange.fetch()
    rank = lax.axis_index("ctx")
    steps = (3, 2, 1, 0)
    places = [rank ^ step if ranks == 4 else jnp.int32(index) for index, step in enumerate(steps)]
    back = {}

    def first_part(index, step):
        query_grad, rel_grad, own_key_grad, own_value_grad, key_grad, value_grad = back[step]
        own_grad = jnp.concatenate([own_key_grad, own_value_grad], axis=1)
        main_grad = jnp.concatenate([key_grad, value_grad], axis=1)
        return jnp.concatenate(
            [
                dot_tn(lines, query_grad),
                dot_tn(lines, rel_grad),
                dot_tn(own_lines, own_grad) + dot_tn(main_lines, main_grad),
            ],
            axis=1,
        )

    first = Exchange(ranks, first_part)
    for turn, step in enumerate(steps):
        results = self_backward(
            places[turn].reshape(1),
            own_blocks,
            own,
            query,
            own_keys,
            own_values,
            keys,
            values,
            hot,
            mixed,
            grad_mixed,
            probs,
            own_probs,
        )
        if turn < 3:
            grad_mixed, results = tie(grad_mixed, results)
        back[step] = [flat(value) for value in results]
        if turn == 0 and ranks == 4:
            first.begin(False)
            grad_mixed = hold(grad_mixed, first)
        if turn == 1 and ranks == 4:
            first.turn()
            grad_mixed = hold(grad_mixed, first)
            first.fetch()
        if turn == 2:
            if ranks == 4:
                first.late()
            grad_mixed = hold(grad_mixed, centre, memory_exchange)
            centre_total = centre.end().astype(BF16)
            encoded_grad = memory_exchange.end()
            grad_mixed, centre_total = tie(grad_mixed, centre_total)
            if ranks == 4:
                side, partner = first.values
                grad_mixed, partner = tie(grad_mixed, partner)
                first.values = (side, swap(partner))
            centre_piece = scatter(centre_total)
    joined = [jnp.concatenate(values, axis=1) for values in zip(*(back[step] for step in steps))]
    query_grad, rel_grad, own_key_grad, own_value_grad, key_grad, value_grad = joined
    if ranks == 4:
        back[0][0] = hold(back[0][0], first)
        first_total = first.end().astype(BF16)
        key_grad, own_key_grad, first_total = tie(key_grad, own_key_grad, first_total)
    else:
        whole = column_part(
            ranks,
            [(lines, query_grad)],
            [(lines, rel_grad)],
            [(own_lines, own_key_grad), (main_lines, key_grad)],
            [(own_lines, own_value_grad), (main_lines, value_grad)],
        )
        first = Exchange(ranks, whole)
        first.begin()
        first_total = first.end().astype(BF16)
    first_piece = scatter(first_total)

    def reorder(weight):
        columns = weight.shape[1] // len(steps)
        return jnp.concatenate(
            [
                lax.dynamic_slice_in_dim(weight, index * columns, columns, axis=1)
                for index in places
            ],
            axis=1,
        )

    w_query, w_rel, w_key, w_value = (
        reorder(weight) for weight in (w_query, w_rel, w_key, w_value)
    )
    main_grad = (dot_nt(key_grad, w_key) + dot_nt(value_grad, w_value)).astype(BF16)
    main_grad = jnp.einsum(
        "mu,nmd->nud", order, main_grad.reshape(main_shape), preferred_element_type=F32
    ).astype(BF16)
    main_exchange = Exchange(ranks, block_part(ranks, main_grad))
    main_exchange.begin()
    main_exchange.turn()
    main_exchange.fetch()
    own_grad = dot_nt(own_key_grad, w_key) + dot_nt(own_value_grad, w_value)
    grad_lines = grad_one + dot_nt(query_grad, w_query)
    grad_lines = grad_lines + dot_nt(rel_grad, w_rel)
    grad_lines = grad_lines.reshape(shape) + jnp.concatenate(
        [main_exchange.end()[None], own_grad.reshape(own_shape)], axis=0
    )
    grad_hidden = jnp.transpose(grad_lines, (1, 2, 0, 3))
    norms = total_over(total_over(norms, "ctx", ranks), "fsdp", shards)
    count = norms.shape[1] // shards
    norms = lax.dynamic_slice_in_dim(norms, lax.axis_index("fsdp") * count, count, axis=1)
    gain_one, shift_one, gain_two, shift_two, gain_three, shift_three = (
        norms[index] for index in range(6)
    )
    pieces = collect(ranks, ffn_piece)
    columns = width // ranks
    cut = layers * columns
    w_inner_grad = columns_of(pieces, 0, cut)
    w_outer_grad = jnp.concatenate(
        [columns_of(pieces, cut + layer * columns, columns) for layer in range(layers)], axis=0
    )
    pieces = collect(ranks, centre_piece)
    w_out_grad, c_query_grad, c_key_grad, c_value_grad, c_out_grad = (
        columns_of(pieces, start * columns, columns) for start in range(5)
    )
    pieces = collect(ranks, first_piece)
    rel_columns = w_rel.shape[1] // ranks
    w_query_grad = columns_of(pieces, 0, columns)
    w_rel_grad = columns_of(pieces, columns, rel_columns)
    w_key_grad = columns_of(pieces, columns + rel_columns, columns)
    w_value_grad = columns_of(pieces, 2 * columns + rel_columns, columns)
    return (
        output,
        grad_hidden,
        encoded_grad,
        w_query_grad,
        w_key_grad,
        w_value_grad,
        bucket_major(w_rel_grad),
        w_out_grad,
        gain_one,
        shift_one,
        c_query_grad,
        c_key_grad,
        c_value_grad,
        c_out_grad,
        gain_two,
        shift_two,
        w_inner_grad,
        w_outer_grad,
        gain_three,
        shift_three,
    )


def solution(mesh):
    matrix, vector = P("fsdp", None), P("fsdp")
    rows = P("fsdp", "ctx", None, None)
    weights = (matrix,) * 5 + (vector,) * 2 + (matrix,) * 4 + (vector,) * 2 + (matrix,) * 2
    weights = weights + (vector,) * 2
    in_specs = (rows, P("fsdp", "ctx", None), P(), P()) + weights + (rows,)
    out_specs = (rows, rows, P("fsdp", "ctx", None)) + weights
    return jax.shard_map(
        functools.partial(body, mesh.shape["ctx"], mesh.shape["fsdp"]),
        mesh=mesh,
        in_specs=in_specs,
        out_specs=out_specs,
        check_vma=False,
    )
```

```python
import functools
import jax
import jax.numpy as jnp
from jax import lax
from jax.sharding import PartitionSpec as P
from jax.experimental import pallas as pl
from jax.experimental.pallas import tpu as pltpu

HEAD_DIM = 64
BUCKETS = 32
BLK = 32
CHUNK = 256
FILLER = -1e30
SCALE = HEAD_DIM ** (-0.5)
LIMIT = 60 * 1024 * 1024
F32 = jnp.float32
BF16 = jnp.bfloat16


def dot_nt(left, right):
    return lax.dot_general(left, right, (((1,), (1,)), ((), ())), preferred_element_type=F32)


def dot_tn(left, right):
    return lax.dot_general(left, right, (((0,), (0,)), ((), ())), preferred_element_type=F32)


def dot_nn(left, right):
    return jnp.dot(left, right, preferred_element_type=F32)


def low_lanes(rows):
    return lax.broadcasted_iota(jnp.int32, (rows, 128), 1) < HEAD_DIM


def pair_rows(value, low):
    zero = jnp.zeros_like(value)
    return jnp.concatenate([jnp.where(low, value, zero), jnp.where(low, zero, value)], axis=0)


def self_parts(slot, pair, query_ref, own_key_ref, own_value_ref):
    rows = pl.ds(pl.multiple_of(slot * BLK, BLK), BLK)
    lanes = slice(128 * pair, 128 * (pair + 1))
    total = query_ref.shape[0] * BLK
    low = low_lanes(total)
    query = query_ref[:, 0, rows, lanes].reshape(total, 128)
    pairs = pair_rows(query, low) * jnp.asarray(SCALE, BF16)
    zero = jnp.zeros((BLK, 128), F32)
    own_key = own_key_ref[:, 0, rows, lanes].reshape(total - BLK, 128).astype(F32)
    own_key = jnp.concatenate([zero, own_key], axis=0)
    own_value = own_value_ref[:, 0, rows, lanes].reshape(total - BLK, 128).astype(F32)
    own_value = jnp.concatenate([zero, own_value], axis=0)
    return rows, lanes, low, pairs, own_key, own_value


def slot_pairs(blocks, seq, work):
    def step(place, carry):
        first, second = blocks[2 * place], blocks[2 * place + 1]
        turned = (first > second).astype(jnp.int32)
        near, far = 2 * place + turned, 2 * place + 1 - turned
        near_block, far_block = jnp.minimum(first, second), jnp.maximum(first, second)
        whole = seq // CHUNK
        count = (near_block * BLK) // CHUNK + 1
        for parts in range(1, whole // 2 + 1):

            @pl.when(count == parts)
            def _():
                work(
                    [
                        (slot, block, pair, chunks * CHUNK)
                        for slot, block, chunks in (
                            (near, near_block, parts),
                            (far, far_block, whole + 1 - parts),
                        )
                        for pair in range(2)
                    ]
                )

        return carry

    lax.fori_loop(0, blocks.shape[0] // 2, step, 0)


def self_forward_kernel(
    blocks,
    own_ref,
    query_ref,
    rel_ref,
    own_key_ref,
    own_value_ref,
    key_ref,
    value_ref,
    index_ref,
    out_ref,
    prob_ref,
    own_prob_ref,
):
    seq = key_ref.shape[1]
    streams = query_ref.shape[0]
    total = streams * BLK

    def scored(slot, block, pair, width):
        rows, lanes, low, pairs, own_key, own_value = self_parts(
            slot, pair, query_ref, own_key_ref, own_value_ref
        )
        span = slice(seq - width, seq)
        rel = rel_ref[:, 0, rows, :].reshape(total, 128).astype(F32)
        first = pltpu.roll(rel, 64, 1) if pair else rel
        table = jnp.concatenate([first, pltpu.roll(rel, 32 if pair else 96, 1)], axis=0)
        lane = lax.broadcasted_iota(jnp.int32, (2 * total, 128), 1)
        own = jnp.where(lane == own_ref[0], table, 0.0)
        own = own + pairs.astype(F32) * jnp.concatenate([own_key, own_key], axis=0)
        own = jnp.sum(own, axis=1, keepdims=True)
        row = lax.broadcasted_iota(jnp.int32, (2 * total, 1), 0)
        main = jnp.logical_or(row < BLK, jnp.logical_and(row >= total, row < total + BLK))
        own = jnp.where(main, FILLER, own)
        index = index_ref[rows, span]
        bias = [
            jnp.take_along_axis(
                table,
                jnp.concatenate([index[:, start : start + 128]] * (2 * streams), axis=0),
                axis=1,
            )
            for start in range(0, width, 128)
        ]
        scores = dot_nt(pairs, key_ref[0, span, lanes]) + jnp.concatenate(bias, axis=1)
        column = lax.broadcasted_iota(jnp.int32, (2 * total, CHUNK), 1)
        seen = column >= width - BLK * (block + 1)
        first = jnp.where(seen, scores[:, :CHUNK], FILLER)
        scores = first if width == CHUNK else jnp.concatenate([first, scores[:, CHUNK:]], axis=1)
        top = jnp.maximum(jnp.max(scores, axis=1, keepdims=True), own)
        return scores, own, top, own_value

    def work(items):
        stage = [scored(*item) for item in items]
        stage = [
            (jnp.exp(scores - top), jnp.exp(own - top), own_value)
            for scores, own, top, own_value in stage
        ]
        stage = [
            (weights, own, 1.0 / (jnp.sum(weights, axis=1, keepdims=True) + own), own_value)
            for weights, own, own_value in stage
        ]
        low = low_lanes(total)
        for (slot, block, pair, width), (weights, own, inverse, own_value) in zip(items, stage):
            rows = pl.ds(pl.multiple_of(slot * BLK, BLK), BLK)
            lanes = slice(128 * pair, 128 * (pair + 1))
            span = slice(seq - width, seq)
            probs = (weights * inverse).astype(BF16)
            prob_ref[0, pair, slot, :, span] = probs
            own_prob = own * inverse
            own_prob_ref[0, pair, slot] = jnp.broadcast_to(own_prob, (2 * total, 128)).astype(BF16)
            mixed = dot_nn(probs, value_ref[0, span, lanes])
            result = jnp.where(
                low,
                mixed[:total] + own_prob[:total] * own_value,
                mixed[total:] + own_prob[total:] * own_value,
            )
            out_ref[:, 0, rows, lanes] = result.astype(BF16).reshape(streams, BLK, 128)

    slot_pairs(blocks, seq, work)


def self_backward_kernel(
    group,
    blocks,
    own_ref,
    query_ref,
    own_key_ref,
    own_value_ref,
    key_ref,
    value_ref,
    hot_ref,
    out_ref,
    grad_ref,
    prob_ref,
    own_prob_ref,
    grad_query_ref,
    grad_rel_ref,
    grad_own_key_ref,
    grad_own_value_ref,
    grad_key_ref,
    grad_value_ref,
    key_total,
    value_total,
):
    seq = key_ref.shape[1]
    streams = query_ref.shape[0]
    total = streams * BLK
    key_total[...] = jnp.zeros_like(key_total)
    value_total[...] = jnp.zeros_like(value_total)

    def scored(slot, block, pair, width):
        rows, lanes, low, pairs, own_key, own_value = self_parts(
            slot, pair, query_ref, own_key_ref, own_value_ref
        )
        span = slice(seq - width, seq)
        grads = pair_rows(grad_ref[:, 0, rows, lanes].reshape(total, 128), low)
        wide = grads.astype(F32)
        mixed = out_ref[:, 0, rows, lanes].reshape(total, 128).astype(F32)
        delta = jnp.sum(wide * jnp.concatenate([mixed, mixed], axis=0), axis=1, keepdims=True)
        grad_own = jnp.sum(
            wide * jnp.concatenate([own_value, own_value], axis=0), axis=1, keepdims=True
        )
        own_prob = own_prob_ref[0, pair, slot].astype(F32)
        grad_own = own_prob * (grad_own - delta)
        part = grad_own * pairs.astype(F32)
        part = (part[:total] + part[total:])[BLK:]
        grad_own_key_ref[:, 0, rows, lanes] = part.astype(BF16).reshape(streams - 1, BLK, 128)
        part = own_prob * wide
        part = (part[:total] + part[total:])[BLK:]
        grad_own_value_ref[:, 0, rows, lanes] = part.astype(BF16).reshape(streams - 1, BLK, 128)
        probs = prob_ref[0, pair, slot, :, span]
        grad_probs = dot_nt(grads, value_ref[0, span, lanes])
        grad_scores = probs.astype(F32) * (grad_probs - delta)
        return pairs, grads, own_key, grad_own, probs, grad_scores

    def skew(block, width, grad_scores, grad_own):
        pad = jnp.zeros((BLK, 128), F32)
        skewed = []
        for start in range(0, 2 * total, BLK):
            piece = jnp.concatenate([grad_scores[start : start + BLK], pad], axis=1)
            skewed.append(pltpu.roll(piece, 0, 1, stride=1, stride_axis=0).astype(BF16))
        begin = pl.multiple_of(BLK * (block + 1) - width + CHUNK, BLK)
        sums = dot_nn(jnp.concatenate(skewed, axis=0), hot_ref[pl.ds(begin, width + 128), :])
        lane = lax.broadcasted_iota(jnp.int32, (2 * total, 128), 1)
        return sums + jnp.where(lane == own_ref[0], grad_own, 0.0)

    def work(items):
        stage = [scored(*item) for item in items]
        low = low_lanes(total)
        sums = []
        for (slot, block, pair, width), values in zip(items, stage):
            pairs, grads, own_key, grad_own, probs, grad_scores = values
            rows = pl.ds(pl.multiple_of(slot * BLK, BLK), BLK)
            lanes = slice(128 * pair, 128 * (pair + 1))
            span = slice(seq - width, seq)
            low_scores = grad_scores.astype(BF16)
            value_total[span, lanes] += dot_tn(probs, grads)
            key_total[span, lanes] += dot_tn(low_scores, pairs)
            moved = dot_nn(low_scores, key_ref[0, span, lanes])
            moved = jnp.where(
                low,
                moved[:total] + grad_own[:total] * own_key,
                moved[total:] + grad_own[total:] * own_key,
            )
            grad_query_ref[:, 0, rows, lanes] = (
                (moved * SCALE).astype(BF16).reshape(streams, BLK, 128)
            )
            sums.append(skew(block, width, grad_scores, grad_own))
        for place in range(0, len(items), 2):
            slot = items[place][0]
            rows = pl.ds(pl.multiple_of(slot * BLK, BLK), BLK)
            result = sums[place][:total] + pltpu.roll(sums[place][total:], BUCKETS, 1)
            result = result + pltpu.roll(sums[place + 1][:total], 2 * BUCKETS, 1)
            result = result + pltpu.roll(sums[place + 1][total:], 3 * BUCKETS, 1)
            grad_rel_ref[:, 0, rows, :] = result.astype(BF16).reshape(streams, BLK, 128)

    slot_pairs(blocks, seq, work)
    grad_key_ref[0] = key_total[...].astype(BF16)
    grad_value_ref[0] = value_total[...].astype(BF16)


def group_spec(streams, rows, lanes):
    return pl.BlockSpec((streams, 1, rows, lanes), lambda n, g: (0, n, 0, g))


def full_spec(rows, lanes):
    return pl.BlockSpec((1, rows, lanes), lambda n, g: (n, 0, g))


def smem_spec():
    return pl.BlockSpec(memory_space=pltpu.SMEM)


def estimate(flops, moved):
    return pl.CostEstimate(flops=int(flops), bytes_accessed=int(moved), transcendentals=0)


def prob_spec(slots, total, width):
    return pl.BlockSpec((1, 2, slots, total, width), lambda n, g: (n, g, 0, 0, 0))


def whole_spec(value):
    return pl.BlockSpec(value.shape, lambda n, g: (0,) * value.ndim)


def self_forward(blocks, own, query, rel, own_key, own_value, keys, values, index):
    streams, seqs, rows, width = query.shape
    seq = keys.shape[1]
    slots = rows // BLK
    total = 2 * streams * BLK
    return pl.pallas_call(
        self_forward_kernel,
        grid=(seqs, width // 256),
        in_specs=[
            smem_spec(),
            smem_spec(),
            group_spec(streams, rows, 256),
            group_spec(streams, rows, 128),
            group_spec(streams - 1, rows, 256),
            group_spec(streams - 1, rows, 256),
            full_spec(seq, 256),
            full_spec(seq, 256),
            whole_spec(index),
        ],
        out_specs=[
            group_spec(streams, rows, 256),
            prob_spec(slots, total, seq),
            prob_spec(slots, total, 128),
        ],
        out_shape=[
            jax.ShapeDtypeStruct(query.shape, BF16),
            jax.ShapeDtypeStruct((seqs, width // 128, slots, total, seq), BF16),
            jax.ShapeDtypeStruct((seqs, width // 128, slots, total, 128), BF16),
        ],
        compiler_params=pltpu.CompilerParams(vmem_limit_bytes=LIMIT),
        cost_estimate=estimate(88e9, 80e6),
        name="self_forward",
    )(blocks, own, query, rel, own_key, own_value, keys, values, index)


def self_backward(
    group, blocks, own, query, own_key, own_value, keys, values, hot, mixed, grad, probs, own_probs
):
    streams, seqs, rows, width = query.shape
    seq = keys.shape[1]
    slots = rows // BLK
    total = 2 * streams * BLK

    def lines(count):
        return pl.BlockSpec((count, 1, rows, 256), lambda n, g, b, o: (0, n, 0, g[0]))

    def result(count, lanes):
        return pl.BlockSpec((count, 1, rows, lanes), lambda n, g, b, o: (0, n, 0, 0))

    def shape(count, lanes):
        return jax.ShapeDtypeStruct((count, seqs, rows, lanes), BF16)

    def stored(lanes):
        return pl.BlockSpec((1, 2, slots, total, lanes), lambda n, g, b, o: (n, g[0], 0, 0, 0))

    memory = pl.BlockSpec((1, seq, 256), lambda n, g, b, o: (n, 0, g[0]))
    memory_result = pl.BlockSpec((1, seq, 256), lambda n, g, b, o: (n, 0, 0))
    memory_shape = jax.ShapeDtypeStruct((seqs, seq, 256), BF16)
    return pl.pallas_call(
        self_backward_kernel,
        grid_spec=pltpu.PrefetchScalarGridSpec(
            num_scalar_prefetch=3,
            grid=(seqs,),
            in_specs=[
                lines(streams),
                lines(streams - 1),
                lines(streams - 1),
                memory,
                memory,
                pl.BlockSpec(hot.shape, lambda n, g, b, o: (0, 0)),
                lines(streams),
                lines(streams),
                stored(seq),
                stored(128),
            ],
            out_specs=[
                result(streams, 256),
                result(streams, 128),
                result(streams - 1, 256),
                result(streams - 1, 256),
                memory_result,
                memory_result,
            ],
            scratch_shapes=[pltpu.VMEM((seq, 256), F32), pltpu.VMEM((seq, 256), F32)],
        ),
        out_shape=[
            shape(streams, 256),
            shape(streams, 128),
            shape(streams - 1, 256),
            shape(streams - 1, 256),
            memory_shape,
            memory_shape,
        ],
        compiler_params=pltpu.CompilerParams(vmem_limit_bytes=LIMIT),
        cost_estimate=estimate(27e9, 25e6),
        name="self_backward",
    )(group, blocks, own, query, own_key, own_value, keys, values, hot, mixed, grad, probs, own_probs)


def cross_forward_kernel(query_ref, key_ref, value_ref, out_ref, prob_ref):
    rows = query_ref.shape[2]
    low = low_lanes(rows)
    for pair in range(2):
        lanes = slice(128 * pair, 128 * pair + 128)
        pairs = pair_rows(query_ref[0, 0, :, lanes], low) * jnp.asarray(SCALE, BF16)
        scores = dot_nt(pairs, key_ref[0, :, lanes])
        top = jnp.max(scores, axis=1, keepdims=True)
        weights = jnp.exp(scores - top)
        inverse = 1.0 / jnp.sum(weights, axis=1, keepdims=True)
        probs = (weights * inverse).astype(BF16)
        prob_ref[0, 0, pair] = probs
        mixed = dot_nn(probs, value_ref[0, :, lanes])
        out_ref[0, 0, :, lanes] = jnp.where(low, mixed[:rows], mixed[rows:]).astype(BF16)


def cross_backward_kernel(
    query_ref,
    key_ref,
    value_ref,
    out_ref,
    grad_ref,
    prob_ref,
    grad_query_ref,
    grad_key_ref,
    grad_value_ref,
    key_total,
    value_total,
):
    rows = query_ref.shape[2]
    low = low_lanes(rows)
    stream = pl.program_id(2)

    @pl.when(stream == 0)
    def _():
        key_total[...] = jnp.zeros_like(key_total)
        value_total[...] = jnp.zeros_like(value_total)

    for pair in range(2):
        lanes = slice(128 * pair, 128 * pair + 128)
        pairs = pair_rows(query_ref[0, 0, :, lanes], low) * jnp.asarray(SCALE, BF16)
        keys = key_ref[0, :, lanes]
        grads = pair_rows(grad_ref[0, 0, :, lanes], low)
        mixed = out_ref[0, 0, :, lanes].astype(F32)
        delta = jnp.sum(
            grads.astype(F32) * jnp.concatenate([mixed, mixed], axis=0), axis=1, keepdims=True
        )
        probs = prob_ref[0, 0, pair]
        grad_probs = dot_nt(grads, value_ref[0, :, lanes])
        grad_scores = (probs.astype(F32) * (grad_probs - delta)).astype(BF16)
        value_total[:, lanes] += dot_tn(probs, grads)
        key_total[:, lanes] += dot_tn(grad_scores, pairs)
        moved = dot_nn(grad_scores, keys) * SCALE
        grad_query_ref[0, 0, :, lanes] = jnp.where(low, moved[:rows], moved[rows:]).astype(BF16)

    @pl.when(stream == pl.num_programs(2) - 1)
    def _():
        grad_key_ref[0] = key_total[...].astype(BF16)
        grad_value_ref[0] = value_total[...].astype(BF16)


def stream_spec(rows):
    return pl.BlockSpec((1, 1, rows, 256), lambda n, g, s: (s, n, 0, g))


def memory_spec(rows):
    return pl.BlockSpec((1, rows, 256), lambda n, g, s: (n, 0, g))


def cross_prob_spec(rows, memory):
    return pl.BlockSpec((1, 1, 2, 2 * rows, memory), lambda n, g, s: (s, n, g, 0, 0))


def cross_forward(query, keys, values):
    streams, seqs, rows, width = query.shape
    memory = keys.shape[1]
    return pl.pallas_call(
        cross_forward_kernel,
        grid=(seqs, width // 256, streams),
        in_specs=[stream_spec(rows), memory_spec(memory), memory_spec(memory)],
        out_specs=[stream_spec(rows), cross_prob_spec(rows, memory)],
        out_shape=[
            jax.ShapeDtypeStruct(query.shape, BF16),
            jax.ShapeDtypeStruct((streams, seqs, width // 128, 2 * rows, memory), BF16),
        ],
        compiler_params=pltpu.CompilerParams(vmem_limit_bytes=LIMIT),
        cost_estimate=estimate(38e9, 40e6),
        name="cross_forward",
    )(query, keys, values)


def cross_backward(query, keys, values, mixed, grad, probs):
    streams, seqs, rows, width = query.shape
    memory = keys.shape[1]
    return pl.pallas_call(
        cross_backward_kernel,
        grid=(seqs, width // 256, streams),
        in_specs=[
            stream_spec(rows),
            memory_spec(memory),
            memory_spec(memory),
            stream_spec(rows),
            stream_spec(rows),
            cross_prob_spec(rows, memory),
        ],
        out_specs=[stream_spec(rows), memory_spec(memory), memory_spec(memory)],
        out_shape=[
            jax.ShapeDtypeStruct(query.shape, BF16),
            jax.ShapeDtypeStruct(keys.shape, BF16),
            jax.ShapeDtypeStruct(keys.shape, BF16),
        ],
        scratch_shapes=[pltpu.VMEM((memory, 256), F32), pltpu.VMEM((memory, 256), F32)],
        compiler_params=pltpu.CompilerParams(vmem_limit_bytes=LIMIT),
        cost_estimate=estimate(47e9, 50e6),
        name="cross_backward",
    )(query, keys, values, mixed, grad, probs)


def bucket_index(own_blocks, bucket_table, seq):
    span = bucket_table.shape[0]
    front = seq - BLK
    length = 2 * seq + BLK
    line = jnp.zeros((length,), jnp.int32).at[front : front + span].set(bucket_table)
    flat = jnp.tile(line, BLK + 1)[: BLK * (length + 1)]
    skew = flat.reshape(BLK, length + 1)
    parts = [
        lax.dynamic_slice_in_dim(skew, own_blocks[slot] * BLK, seq, axis=1)
        for slot in range(own_blocks.shape[0])
    ]
    return jnp.concatenate(parts, axis=0)


def bucket_hots(bucket_table, seq, front):
    span = bucket_table.shape[0]
    depth = CHUNK + seq + 128
    line = jnp.full((front + span + depth,), -1, jnp.int32)
    line = line.at[front : front + span].set(bucket_table)[:depth]
    lane = jnp.arange(128, dtype=jnp.int32)
    return (line[:, None] == lane[None, :]).astype(BF16)


EPSILON = 1e-05
FULL = ("fsdp", "ctx")


PARTNER = [(0, 1), (1, 0), (2, 3), (3, 2)]
ACROSS = [(0, 2), (2, 0), (1, 3), (3, 1)]


def gather(shard, ranks):
    rows = shard.shape[0] // ranks
    piece = lax.dynamic_slice_in_dim(shard, lax.axis_index("ctx") * rows, rows)
    return lax.all_gather(piece, FULL, axis=0, tiled=True)


def swap(value):
    return lax.ppermute(value, "ctx", PARTNER)


def pass_across(value):
    return lax.ppermute(value, "ctx", ACROSS)


def tie(*values):
    return lax.optimization_barrier(values)


def spread(piece):
    across = pass_across(piece)
    return piece, swap(piece), across, swap(across)


def place_kernel(rank, first, second, third, fourth, out_ref):
    for step, ref in enumerate((first, second, third, fourth)):

        @pl.when((rank[0] ^ step) == pl.program_id(0))
        def _():
            out_ref[:, 0] = ref[...]


def place(pieces):
    outer, rows, columns = pieces[0].shape
    return pl.pallas_call(
        place_kernel,
        grid=(4,),
        in_specs=[smem_spec()] + [whole_block(piece) for piece in pieces],
        out_specs=pl.BlockSpec((outer, 1, rows, columns), lambda step: (0, step, 0, 0)),
        out_shape=jax.ShapeDtypeStruct((outer, 4, rows, columns), pieces[0].dtype),
        compiler_params=pltpu.CompilerParams(vmem_limit_bytes=LIMIT),
        cost_estimate=estimate(0, 8 * pieces[0].size * 2),
        name="place",
    )(lax.axis_index("ctx").reshape(1), *pieces)


def whole_block(value):
    return pl.BlockSpec(
        value.shape, lambda step: (0,) * value.ndim, pipeline_mode=pl.Buffered(1)
    )


def gather_half(shard, ranks):
    if ranks != 4:
        return gather(shard, ranks)
    rows = shard.shape[0] // ranks
    piece = lax.dynamic_slice_in_dim(shard, lax.axis_index("ctx") * rows, rows)
    return lax.all_gather(piece, "fsdp", axis=0, tiled=False)


def gather_pass(piece, ranks):
    if ranks != 4:
        return (piece,)
    return piece, swap(piece), pass_across(piece)


def gather_rest(pieces, ranks):
    if ranks != 4:
        return pieces[0]
    piece, partner, across = pieces
    return place((piece, partner, across, swap(across))).reshape(-1, piece.shape[2])


def gather_rows(value, ranks):
    if ranks != 4:
        return lax.all_gather(value, "ctx", axis=1, tiled=True)
    return place(spread(value)).reshape(value.shape[0], -1, value.shape[2])


def column_part(count, *groups):
    def part(index, step):
        parts = []
        for group in groups:
            total = 0.0
            for left, right in group:
                columns = right.shape[1] // count
                right = lax.dynamic_slice_in_dim(right, index * columns, columns, axis=1)
                total = total + dot_tn(left, right)
            parts.append(total)
        return parts[0] if len(parts) == 1 else jnp.concatenate(parts, axis=1)

    return part


def block_part(count, value):
    rows = value.shape[1] // count

    def part(index, step):
        return lax.dynamic_slice_in_dim(value, index * rows, rows, axis=1).astype(F32)

    return part


class Exchange:
    def __init__(self, ranks, part):
        self.ranks = ranks
        self.part = part
        self.rank = lax.axis_index("ctx")

    def begin(self, both=True):
        if self.ranks != 4:
            every = [self.part(index, index).astype(BF16) for index in range(self.ranks)]
            self.values = (jnp.stack(every),)
            return
        self.values = (self.part(self.rank ^ 3, 3).astype(BF16),)
        if both:
            self.late()

    def late(self):
        self.values = self.values + (self.part(self.rank ^ 1, 1).astype(BF16),)

    def turn(self):
        if self.ranks != 4:
            return
        corner, partner = swap(self.values[0]), self.values[1:]
        side = (self.part(self.rank ^ 2, 2) + corner.astype(F32)).astype(BF16)
        self.values = (side,) + tuple(swap(value) for value in partner)

    def fetch(self):
        if self.ranks == 4:
            self.values = (pass_across(self.values[0]),) + self.values[1:]

    def end(self):
        if self.ranks != 4:
            mine = lax.psum_scatter(self.values[0], "ctx", scatter_dimension=0, tiled=True)
            return mine[0].astype(F32)
        side, partner = self.values
        return self.part(self.rank, 0) + partner.astype(F32) + side.astype(F32)


def hold(value, *items):
    packed = [item.values if isinstance(item, Exchange) else item for item in items]
    value, packed = tie(value, packed)
    for item, new in zip(items, packed):
        if isinstance(item, Exchange):
            item.values = new
    others = [new for item, new in zip(items, packed) if not isinstance(item, Exchange)]
    return (value, *others) if others else value


def scatter(total):
    return lax.psum_scatter(total.astype(BF16), "fsdp", scatter_dimension=0, tiled=True)


def collect(ranks, piece):
    if ranks != 4:
        whole = lax.all_gather(piece, "ctx", axis=0, tiled=False)
        return [whole[index].astype(F32) for index in range(ranks)]
    rank = lax.axis_index("ctx")
    pieces = spread(piece)
    ordered = []
    for index in range(4):
        chosen = pieces[3]
        for step in range(3):
            chosen = jnp.where((rank ^ step) == index, pieces[step], chosen)
        ordered.append(chosen.astype(F32))
    return ordered


def columns_of(pieces, start, columns):
    return jnp.concatenate([piece[:, start : start + columns] for piece in pieces], axis=1)


def total_over(value, axis, size):
    step = 1
    while step < size:
        value = value + lax.ppermute(value, axis, [(index, index ^ step) for index in range(size)])
        step *= 2
    return value


def flat(value):
    return value.reshape(-1, value.shape[-1])


def normalize(values):
    average = jnp.mean(values, axis=-1, keepdims=True)
    centred = values - average
    variance = jnp.mean(centred * centred, axis=-1, keepdims=True)
    rate = lax.rsqrt(variance + EPSILON)
    return centred * rate, rate


def norm_back(grad, normal, rate, gain):
    inner = grad * gain
    first = jnp.mean(inner, axis=-1, keepdims=True)
    second = jnp.mean(inner * normal, axis=-1, keepdims=True)
    back = (inner - first - normal * second) * rate
    return back, jnp.sum(grad * normal, axis=0), jnp.sum(grad, axis=0)


def gelu_parts(inner):
    share = 0.5 * (1.0 + lax.erf(inner * (0.5**0.5)))
    slope = share + inner * jnp.exp(-0.5 * inner * inner) * ((0.5 / jnp.pi) ** 0.5)
    return (inner * share).astype(BF16), slope.astype(BF16)


def head_major(weight):
    rows, width = weight.shape
    return weight.reshape(rows, BUCKETS, width // BUCKETS).transpose(0, 2, 1).reshape(rows, width)


def bucket_major(weight):
    rows, width = weight.shape
    return weight.reshape(rows, width // BUCKETS, BUCKETS).transpose(0, 2, 1).reshape(rows, width)


def body(
    ranks,
    shards,
    hidden,
    encoded,
    assign,
    bucket_table,
    w_query,
    w_key,
    w_value,
    w_rel,
    w_out,
    gain_one,
    shift_one,
    c_query,
    c_key,
    c_value,
    c_out,
    gain_two,
    shift_two,
    w_inner,
    w_outer,
    gain_three,
    shift_three,
    cotangent,
):
    seqs, rows, streams, width = hidden.shape
    seq = rows * ranks
    rank = lax.axis_index("ctx")
    slots = rows // BLK
    own_blocks = lax.dynamic_slice_in_dim(assign, rank * slots, slots)
    own = bucket_table[BLK - 1 : BLK]
    index = bucket_index(own_blocks, bucket_table, seq)
    hot = bucket_hots(bucket_table, seq, CHUNK)
    places = (assign[:, None] * BLK + jnp.arange(BLK, dtype=jnp.int32)[None, :]).reshape(-1)
    order = (places[None, :] == (seq - 1 - jnp.arange(seq, dtype=jnp.int32))[:, None]).astype(BF16)

    stacked = jnp.transpose(hidden, (2, 0, 1, 3))
    shape = stacked.shape
    parts = [w_key, w_value, w_query, head_major(w_rel)]
    full = gather(jnp.concatenate(parts, axis=1), ranks)
    main = gather_rows(hidden[:, :, 0, :], ranks)
    memory = gather_rows(encoded, ranks)
    main = jnp.einsum("mu,nud->nmd", order, main, preferred_element_type=F32).astype(BF16)
    norms = [gain_one, shift_one, gain_two, shift_two, gain_three, shift_three]
    norms = jnp.pad(jnp.stack(norms, axis=1), ((0, 0), (0, 122)))
    middle = jnp.concatenate([w_out, c_query, c_key, c_value, c_out, norms], axis=1)
    full, main, memory, stacked, middle, w_inner, w_outer = tie(
        full, main, memory, stacked, middle, w_inner, w_outer
    )
    middle = gather_pass(gather_half(middle, ranks), ranks)
    w_inner = gather_half(w_inner, ranks)
    w_outer = gather_half(w_outer, ranks)
    w_key, w_value, w_query = (full[:, start : start + width] for start in range(0, 3 * width, width))
    w_rel = full[:, 3 * width :]
    lines = flat(stacked)
    own_shape = (streams - 1,) + shape[1:]
    own_lines = flat(stacked[1:])
    main_lines = flat(main)
    main_shape = main.shape
    query = dot_nn(lines, w_query).astype(BF16).reshape(shape)
    rel = dot_nn(lines, w_rel).astype(BF16).reshape(shape[:-1] + (-1,))
    own_keys = dot_nn(own_lines, w_key).astype(BF16).reshape(own_shape)
    own_values = dot_nn(own_lines, w_value).astype(BF16).reshape(own_shape)
    keys = dot_nn(main_lines, w_key).astype(BF16).reshape(main_shape)
    values = dot_nn(main_lines, w_value).astype(BF16).reshape(main_shape)
    mixed, probs, own_probs = self_forward(
        own_blocks, own, query, rel, own_keys, own_values, keys, values, index
    )
    mixed, middle, w_inner = tie(mixed, middle, w_inner)
    w_inner = gather_pass(w_inner, ranks)
    full = gather_rest(middle, ranks)
    w_out, c_query, c_key, c_value, c_out = (
        full[:, start : start + width] for start in range(0, 5 * width, width)
    )
    norms = jnp.transpose(full[:, 5 * width :])[:6].astype(F32)
    gain_one, shift_one, gain_two, shift_two, gain_three, shift_three = (
        norms[index : index + 1] for index in range(6)
    )
    normal_one, rate_one = normalize(lines.astype(F32) + dot_nn(flat(mixed), w_out))
    h_one = normal_one * gain_one + shift_one
    h_one_low = h_one.astype(BF16)
    cross_query = dot_nn(h_one_low, c_query).astype(BF16).reshape(shape)
    cross_query, w_outer = tie(cross_query, w_outer)
    w_outer = gather_pass(w_outer, ranks)
    memory_lines = flat(memory)
    cross_keys = dot_nn(memory_lines, c_key).astype(BF16).reshape(memory.shape)
    cross_values = dot_nn(memory_lines, c_value).astype(BF16).reshape(memory.shape)
    cross_mixed, cross_probs = cross_forward(cross_query, cross_keys, cross_values)
    cross_mixed, w_inner = tie(cross_mixed, w_inner)
    w_inner = gather_rest(w_inner, ranks)
    normal_two, rate_two = normalize(h_one + dot_nn(flat(cross_mixed), c_out))
    h_two = normal_two * gain_two + shift_two
    h_two_low = h_two.astype(BF16)
    active, slope = gelu_parts(dot_nn(h_two_low, w_inner))
    active, w_outer = tie(active, w_outer)
    w_outer = gather_rest(w_outer, ranks)
    normal_three, rate_three = normalize(h_two + dot_nn(active, w_outer))
    output = (normal_three * gain_three + shift_three).astype(BF16)
    output = jnp.transpose(output.reshape(shape), (1, 2, 0, 3))

    grad = flat(jnp.transpose(cotangent, (2, 0, 1, 3))).astype(F32)
    grad_three, gain_three, shift_three = norm_back(grad, normal_three, rate_three, gain_three)
    grad_low = grad_three.astype(BF16)
    outer = Exchange(ranks, column_part(ranks, [(active, grad_low)]))
    outer.begin()
    grad_low = hold(grad_low, outer)
    grad_inner = (dot_nt(grad_low, w_outer) * slope.astype(F32)).astype(BF16)
    inner = Exchange(ranks, column_part(ranks, [(h_two_low, grad_inner)]))
    inner.begin()
    outer.turn()
    grad_inner = hold(grad_inner, inner, outer)
    outer.fetch()
    grad_h_two = grad_three + dot_nt(grad_inner, w_inner)
    grad_two, gain_two, shift_two = norm_back(grad_h_two, normal_two, rate_two, gain_two)
    c_out_low = grad_two.astype(BF16)
    inner.turn()
    grad_low = hold(c_out_low, inner)
    inner.fetch()
    grad_mixed = dot_nt(grad_low, c_out).astype(BF16).reshape(shape)
    cross_query_grad, key_grad, value_grad = cross_backward(
        cross_query, cross_keys, cross_values, cross_mixed, grad_mixed, cross_probs
    )
    cross_query_grad = hold(cross_query_grad, inner, outer)
    inner_total, outer_total = inner.end().astype(BF16), outer.end().astype(BF16)
    cross_query_grad, inner_total, outer_total = tie(cross_query_grad, inner_total, outer_total)
    depth = width // shards
    layers = outer_total.shape[0] // width
    outer_total = outer_total.reshape(shards, layers, depth, -1)
    parts = [outer_total[:, layer].reshape(width, -1) for layer in range(layers)]
    ffn_piece = scatter(jnp.concatenate([inner_total] + parts, axis=1))
    cross_query_grad = flat(cross_query_grad)
    key_grad, value_grad = flat(key_grad), flat(value_grad)
    grad_h_one = grad_two + dot_nt(cross_query_grad, c_query)
    grad_one, gain_one, shift_one = norm_back(grad_h_one, normal_one, rate_one, gain_one)
    grad_low = grad_one.astype(BF16)
    grad_mixed = dot_nt(grad_low, w_out).astype(BF16).reshape(shape)
    centre = Exchange(
        ranks,
        column_part(
            ranks,
            [(flat(mixed), grad_low)],
            [(h_one_low, cross_query_grad)],
            [(memory_lines, key_grad)],
            [(memory_lines, value_grad)],
            [(flat(cross_mixed), c_out_low)],
        ),
    )
    centre.begin()
    encoded_grad = (dot_nt(key_grad, c_key) + dot_nt(value_grad, c_value)).astype(BF16)
    centre.turn()
    memory_exchange = Exchange(ranks, block_part(ranks, encoded_grad.reshape(memory.shape)))
    memory_exchange.begin()
    norms = jnp.stack([gain_one, shift_one, gain_two, shift_two, gain_three, shift_three])
    grad_mixed, norms = hold(grad_mixed, centre, memory_exchange, norms)
    centre.fetch()
    memory_exchange.turn()
    memory_exchange.fetch()
    rank = lax.axis_index("ctx")
    steps = (3, 2, 1, 0)
    places = [rank ^ step if ranks == 4 else jnp.int32(index) for index, step in enumerate(steps)]
    back = {}

    def first_part(index, step):
        query_grad, rel_grad, own_key_grad, own_value_grad, key_grad, value_grad = back[step]
        own_grad = jnp.concatenate([own_key_grad, own_value_grad], axis=1)
        main_grad = jnp.concatenate([key_grad, value_grad], axis=1)
        return jnp.concatenate(
            [
                dot_tn(lines, query_grad),
                dot_tn(lines, rel_grad),
                dot_tn(own_lines, own_grad) + dot_tn(main_lines, main_grad),
            ],
            axis=1,
        )

    first = Exchange(ranks, first_part)
    for turn, step in enumerate(steps):
        results = self_backward(
            places[turn].reshape(1),
            own_blocks,
            own,
            query,
            own_keys,
            own_values,
            keys,
            values,
            hot,
            mixed,
            grad_mixed,
            probs,
            own_probs,
        )
        if turn < 3:
            grad_mixed, results = tie(grad_mixed, results)
        back[step] = [flat(value) for value in results]
        if turn == 0 and ranks == 4:
            first.begin(False)
            grad_mixed = hold(grad_mixed, first)
        if turn == 1 and ranks == 4:
            first.turn()
            grad_mixed = hold(grad_mixed, first)
            first.fetch()
        if turn == 2 and ranks == 4:
            first.late()
            side, partner = first.values
            grad_mixed, partner = tie(grad_mixed, partner)
            first.values = (side, swap(partner))
    joined = [jnp.concatenate(values, axis=1) for values in zip(*(back[step] for step in steps))]
    query_grad, rel_grad, own_key_grad, own_value_grad, key_grad, value_grad = joined
    if ranks == 4:
        back[0][0] = hold(back[0][0], first, centre, memory_exchange)
        centre_total = centre.end().astype(BF16)
        first_total = first.end().astype(BF16)
        key_grad, own_key_grad, first_total, centre_total = tie(
            key_grad, own_key_grad, first_total, centre_total
        )
    else:
        whole = column_part(
            ranks,
            [(lines, query_grad)],
            [(lines, rel_grad)],
            [(own_lines, own_key_grad), (main_lines, key_grad)],
            [(own_lines, own_value_grad), (main_lines, value_grad)],
        )
        first = Exchange(ranks, whole)
        first.begin()
        centre_total = centre.end().astype(BF16)
        first_total = first.end().astype(BF16)
    last_piece = scatter(jnp.concatenate([centre_total, first_total], axis=1))
    encoded_grad = memory_exchange.end()

    def reorder(weight):
        columns = weight.shape[1] // len(steps)
        return jnp.concatenate(
            [
                lax.dynamic_slice_in_dim(weight, index * columns, columns, axis=1)
                for index in places
            ],
            axis=1,
        )

    w_query, w_rel, w_key, w_value = (
        reorder(weight) for weight in (w_query, w_rel, w_key, w_value)
    )
    main_grad = (dot_nt(key_grad, w_key) + dot_nt(value_grad, w_value)).astype(BF16)
    main_grad = jnp.einsum(
        "mu,nmd->nud", order, main_grad.reshape(main_shape), preferred_element_type=F32
    ).astype(BF16)
    main_exchange = Exchange(ranks, block_part(ranks, main_grad))
    main_exchange.begin()
    main_exchange.turn()
    main_exchange.fetch()
    own_grad = dot_nt(own_key_grad, w_key) + dot_nt(own_value_grad, w_value)
    grad_lines = grad_one + dot_nt(query_grad, w_query)
    grad_lines = grad_lines + dot_nt(rel_grad, w_rel)
    grad_lines = grad_lines.reshape(shape) + jnp.concatenate(
        [main_exchange.end()[None], own_grad.reshape(own_shape)], axis=0
    )
    grad_hidden = jnp.transpose(grad_lines, (1, 2, 0, 3))
    norms = total_over(total_over(norms, "ctx", ranks), "fsdp", shards)
    count = norms.shape[1] // shards
    norms = lax.dynamic_slice_in_dim(norms, lax.axis_index("fsdp") * count, count, axis=1)
    gain_one, shift_one, gain_two, shift_two, gain_three, shift_three = (
        norms[index] for index in range(6)
    )
    pieces = collect(ranks, ffn_piece)
    columns = width // ranks
    cut = layers * columns
    w_inner_grad = columns_of(pieces, 0, cut)
    w_outer_grad = jnp.concatenate(
        [columns_of(pieces, cut + layer * columns, columns) for layer in range(layers)], axis=0
    )
    pieces = collect(ranks, last_piece)
    w_out_grad, c_query_grad, c_key_grad, c_value_grad, c_out_grad = (
        columns_of(pieces, start * columns, columns) for start in range(5)
    )
    rel_columns = w_rel.shape[1] // ranks
    start = 5 * columns
    w_query_grad = columns_of(pieces, start, columns)
    w_rel_grad = columns_of(pieces, start + columns, rel_columns)
    w_key_grad = columns_of(pieces, start + columns + rel_columns, columns)
    w_value_grad = columns_of(pieces, start + 2 * columns + rel_columns, columns)
    return (
        output,
        grad_hidden,
        encoded_grad,
        w_query_grad,
        w_key_grad,
        w_value_grad,
        bucket_major(w_rel_grad),
        w_out_grad,
        gain_one,
        shift_one,
        c_query_grad,
        c_key_grad,
        c_value_grad,
        c_out_grad,
        gain_two,
        shift_two,
        w_inner_grad,
        w_outer_grad,
        gain_three,
        shift_three,
    )


def solution(mesh):
    matrix, vector = P("fsdp", None), P("fsdp")
    rows = P("fsdp", "ctx", None, None)
    weights = (matrix,) * 5 + (vector,) * 2 + (matrix,) * 4 + (vector,) * 2 + (matrix,) * 2
    weights = weights + (vector,) * 2
    in_specs = (rows, P("fsdp", "ctx", None), P(), P()) + weights + (rows,)
    out_specs = (rows, rows, P("fsdp", "ctx", None)) + weights
    return jax.shard_map(
        functools.partial(body, mesh.shape["ctx"], mesh.shape["fsdp"]),
        mesh=mesh,
        in_specs=in_specs,
        out_specs=out_specs,
        check_vma=False,
    )
```
